256 devices in a mesh: dp: 32 (over z, x_lo, core), mesh: 8 (over y, x_hi).
Axes of the slice: x: 4 (x_hi: 2, x_lo: 2; x = x_hi * 2 + x_lo), y: 4, z: 8, core: 2. Of those that a mesh axis runs over, the one named last changes fastest.
Arguments:
- node_feats: bfloat16 [32, 512, 512], P('dp', 'mesh'), may hold values from -6 to 6
- edge_feats: bfloat16 [32, 512, 8, 512], P('dp', 'mesh'), may hold values from -6 to 6
- node_cot: bfloat16 [32, 512, 512], P('dp', 'mesh'), may hold values from -6 to 6
- edge_cot: bfloat16 [32, 512, 8, 512], P('dp', 'mesh'), may hold values from -6 to 6
- w_edge_in: bfloat16 [2, 1536, 512], replicated, may hold values from -0.15625 to 0.15625
- w_edge_out: bfloat16 [2, 512, 512], replicated, may hold values from -0.25 to 0.25
- w_node_in: bfloat16 [2, 1024, 512], replicated, may hold values from -0.1875 to 0.1875
- w_node_out: bfloat16 [2, 512, 512], replicated, may hold values from -0.25 to 0.25
- neighbours: int32 [512, 8], P('mesh'), may hold values from 0 to 95
- send_rows: int32 [8, 32], P('mesh'), may hold values from 0 to 63, as said below
- edge_counts: int32 [512], P('mesh'), may hold values from 1 to 8
- ocean_mask: int32 [512], P('mesh'), may hold values 0 or 1
Outputs:
- grad_nodes: float32 [32, 512, 512], P('dp', 'mesh')
- grad_edges: bfloat16 [32, 512, 8, 512], P('dp', 'mesh')
- grad_edge_in: float32 [2, 1536, 512], P(None, 'dp')
- grad_edge_out: float32 [2, 512, 512], P(None, 'dp')
- grad_node_in: float32 [2, 1024, 512], P(None, 'dp')
- grad_node_out: float32 [2, 512, 512], P(None, 'dp')
The draws below stay inside these ranges and needn't reach their ends.
Inputs may be any that keep to these rules, and one draw needn't show every extreme that they name: `send_rows`: within each partition's row the (32) entries are distinct local rows.
All inputs are finite; a program needn't handle non-finite values. No bound on the sum of `ocean_mask` on one device may be relied on, other than what follows from the above.
Results may differ from the reference program's by a relative error of at most 0.03.
Values may be sent and summed in bfloat16 or wider, within the bound.
A program may use at most 128 MiB of HBM per device.

```python
import jax
import jax.numpy as jnp
from jax import lax

D = 512
K = 8
LAYERS = 2
ND = 64
HALO = 16
SAMPLES = 32
NODES = 512
N_MESH = 8


def draw_send_rows(key, part):
    scores = jax.random.randint(key, (N_MESH, ND), 0, 1 << 20, dtype=jnp.int32) * ND
    scores = scores + jnp.arange(ND, dtype=jnp.int32)[None, :]
    ranking = jnp.argsort(scores, axis=1)
    return ranking[:, :2 * HALO].astype(jnp.int32)


def plant(drawn, key, least, high):
    extent = drawn.shape
    index_at = [jax.random.randint(jax.random.fold_in(key, axis), (), 0, extent[axis]) for axis in range(len(extent))]
    drawn = drawn.at[tuple(index_at)].set(least)
    longest = extent.index(max(extent))
    index_at[longest] = (index_at[longest] + 1) % extent[longest]
    return drawn.at[tuple(index_at)].set(high)


def spiked(drawn, stream_key, source, target, parts, factor):
    def block_of(position):
        return (jnp.arange(drawn.shape[position]) // (drawn.shape[position] // parts)).reshape((-1,) + (1,) * (drawn.ndim - 1 - position))

    one_side = jax.random.permutation(stream_key, parts)[block_of(target)]
    second = (block_of(target) + parts // 2) % parts
    return jnp.where((block_of(source) == one_side) | (block_of(source) == second), factor * drawn, drawn)


def block_levels(rng, extent, cuts, least, top_value):
    gain = 1.0
    for axis_at, shards_of in cuts:
        draws = jax.random.uniform(jax.random.fold_in(jax.random.fold_in(rng, 6), axis_at), (shards_of,), jnp.float32, least / len(cuts), top_value / len(cuts))
        gain = gain * jnp.repeat(jnp.exp(draws), extent[axis_at] // shards_of).reshape((-1,) + (1,) * (len(extent) - 1 - axis_at))
    return gain


def gaussian(key, dims, scale, reach, cuts=(), held_as=jnp.bfloat16):
    array = jax.random.normal(key, dims, jnp.float32) * scale
    if len(cuts) > 0:
        array = block_levels(key, dims, cuts, -0.22, 0.18) * array
    return jnp.clip(array, min=-reach, max=reach).astype(held_as)


def noise_with(stream_key, extent, width, reach, pieces, heavy, held_as=jnp.bfloat16):
    drawn = width * jax.random.normal(stream_key, extent, jnp.float32)
    if pieces:
        drawn = drawn * block_levels(stream_key, extent, pieces, -0.22, 0.18)
    return jnp.clip(spiked(drawn, jax.random.fold_in(stream_key, 3), *heavy), -reach, reach).astype(held_as)


def setup_inputs(seed: int = 0) -> dict:
    arg_keys = jax.random.split(jax.random.key(seed), 13)
    node_feats = noise_with(arg_keys[0], (SAMPLES, NODES, D), 1.0, 6.0, ((0, 32), (1, 8)), (0, 2, 32, 2.75))
    edge_feats = noise_with(arg_keys[1], (SAMPLES, NODES, K, D), 1.0, 6.0, ((0, 32), (1, 8)), (0, 3, 32, 2.75))
    node_cot = gaussian(arg_keys[2], (SAMPLES, NODES, D), 1.0, 6.0, ((0, 32), (1, 8)))
    edge_cot = gaussian(arg_keys[3], (SAMPLES, NODES, K, D), 1.0, 6.0, ((0, 32), (1, 8)))
    w_edge_in = gaussian(arg_keys[4], (LAYERS, 3 * D, D), (3 * D) ** -0.5, 0.15625)
    w_edge_out = gaussian(arg_keys[5], (LAYERS, D, D), D ** -0.5, 0.25)
    w_node_in = gaussian(arg_keys[6], (LAYERS, 2 * D, D), (2 * D) ** -0.5, 0.1875)
    w_node_out = gaussian(arg_keys[7], (LAYERS, D, D), D ** -0.5, 0.25)
    neighbours = plant(jax.random.randint(arg_keys[8], (NODES, K), 0, ND + 2 * HALO), jax.random.fold_in(arg_keys[8], 1), 0, (ND + 2 * HALO) - 1).astype(jnp.int32)
    send_rows = draw_send_rows(jax.random.fold_in(arg_keys[12], 71), 0)
    edge_counts = plant(jax.random.randint(arg_keys[10], (NODES,), 1, K + 1), jax.random.fold_in(arg_keys[10], 1), 1, K).astype(jnp.int32)
    ocean_mask = plant((jax.random.randint(arg_keys[11], (NODES,), 0, 4) < 3).astype(jnp.int32), jax.random.fold_in(arg_keys[11], 1), 0, 1)
    return dict(node_feats=node_feats, edge_feats=edge_feats, node_cot=node_cot, edge_cot=edge_cot, w_edge_in=w_edge_in, w_edge_out=w_edge_out, w_node_in=w_node_in, w_node_out=w_node_out, neighbours=neighbours, send_rows=send_rows, edge_counts=edge_counts, ocean_mask=ocean_mask)


def normalize(values):
    center = lax.optimization_barrier(jnp.mean(values, axis=-1, keepdims=True))
    shifted = values - center
    inverse = lax.rsqrt(lax.optimization_barrier(jnp.mean(shifted * shifted, axis=-1, keepdims=True)) + 1e-05)
    return shifted * inverse

def normalize_back(values, upstream):
    center = lax.optimization_barrier(jnp.mean(values, axis=-1, keepdims=True))
    shifted = values - center
    inverse = lax.rsqrt(lax.optimization_barrier(jnp.mean(shifted * shifted, axis=-1, keepdims=True)) + 1e-05)
    normed = shifted * inverse
    return inverse * (upstream - lax.optimization_barrier(jnp.mean(upstream, axis=-1, keepdims=True)) - normed * lax.optimization_barrier(jnp.mean(upstream * normed, axis=-1, keepdims=True)))

def silu_slope(values):
    sigmoid_val = jax.nn.sigmoid(values)
    return sigmoid_val * (1.0 + values * (1.0 - sigmoid_val))

def forward(nodes, edges, sources, active_slots, wet_ocean_rows, weights):
    edge_in, edge_out, node_in, node_out = weights
    count, slot_count, features = edges.shape
    edge_input = jnp.concatenate([edges, sources, jnp.broadcast_to(nodes[:, None, :], edges.shape)], axis=-1).reshape(count * slot_count, 3 * features)
    pre_edge = jnp.dot(edge_input, edge_in, preferred_element_type=jnp.float32)
    act_edge = jax.nn.silu(pre_edge).astype(jnp.bfloat16)
    pre_edge_out = jnp.dot(act_edge, edge_out, preferred_element_type=jnp.float32)
    update = normalize(pre_edge_out).reshape(count, slot_count, features)
    new_edges = (edges.astype(jnp.float32) + active_slots[:, :, None] * update).astype(jnp.bfloat16)
    message = lax.optimization_barrier(jnp.sum(active_slots[:, :, None] * new_edges.astype(jnp.float32), axis=1)).astype(jnp.bfloat16)
    node_input = jnp.concatenate([nodes, message], axis=-1)
    pre_node = jnp.dot(node_input, node_in, preferred_element_type=jnp.float32)
    act_node = jax.nn.silu(pre_node).astype(jnp.bfloat16)
    pre_node_out = jnp.dot(act_node, node_out, preferred_element_type=jnp.float32)
    new_nodes = (nodes.astype(jnp.float32) + wet_ocean_rows[:, None] * normalize(pre_node_out)).astype(jnp.bfloat16)
    return (new_nodes, new_edges, (edge_input, pre_edge, act_edge, pre_edge_out, node_input, pre_node, act_node, pre_node_out))

def reverse_sweep(saved_activation, grad_nodes, grad_edges, active_slots, wet_ocean_rows, weights):
    edge_in, edge_out, node_in, node_out = weights
    edge_input, pre_edge, act_edge, pre_edge_out, node_input, pre_node, act_node, pre_node_out = saved_activation
    count, slot_count, features = grad_edges.shape
    grad_out = normalize_back(pre_node_out, wet_ocean_rows[:, None] * grad_nodes).astype(jnp.bfloat16)
    grad_node_out = jnp.dot(act_node.T, grad_out, preferred_element_type=jnp.float32)
    grad_act = jnp.dot(grad_out, node_out.T, preferred_element_type=jnp.float32)
    grad_pre = (grad_act * silu_slope(pre_node)).astype(jnp.bfloat16)
    grad_node_in = jnp.dot(node_input.T, grad_pre, preferred_element_type=jnp.float32)
    grad_input = jnp.dot(grad_pre, node_in.T, preferred_element_type=jnp.float32)
    grad_nodes = grad_nodes + grad_input[:, :features]
    grad_edges = grad_edges + active_slots[:, :, None] * grad_input[:, None, features:]
    upstream = (active_slots[:, :, None] * grad_edges).reshape(count * slot_count, features)
    grad_edge_pre_out = normalize_back(pre_edge_out, upstream).astype(jnp.bfloat16)
    grad_edge_out = jnp.dot(act_edge.T, grad_edge_pre_out, preferred_element_type=jnp.float32)
    grad_edge_act = jnp.dot(grad_edge_pre_out, edge_out.T, preferred_element_type=jnp.float32)
    grad_edge_pre = (grad_edge_act * silu_slope(pre_edge)).astype(jnp.bfloat16)
    grad_edge_in = jnp.dot(edge_input.T, grad_edge_pre, preferred_element_type=jnp.float32)
    grad_edge_input = jnp.dot(grad_edge_pre, edge_in.T, preferred_element_type=jnp.float32)
    grad_edge_input = grad_edge_input.reshape(count, slot_count, 3 * features)
    grad_edges = grad_edges + grad_edge_input[:, :, :features]
    source_gradient = grad_edge_input[:, :, features:2 * features]
    grad_nodes = grad_nodes + lax.optimization_barrier(jnp.sum(grad_edge_input[:, :, 2 * features:], axis=1))
    return (grad_nodes, grad_edges, source_gradient, (grad_edge_in, grad_edge_out, grad_node_in, grad_node_out))

def reference(node_feats, edge_feats, node_cot, edge_cot, w_edge_in, w_edge_out, w_node_in, w_node_out, neighbours, send_rows, edge_counts, ocean_mask):
    part_of = (jnp.arange(NODES, dtype=jnp.int32) // ND)[:, None]
    before = (part_of - 1) % N_MESH
    after = (part_of + 1) % N_MESH
    left_slot = jnp.clip(neighbours - ND, 0, HALO - 1).astype(jnp.int32)
    right_slot = jnp.clip(neighbours - ND - HALO, 0, HALO - 1).astype(jnp.int32)
    own_pick = part_of * ND + neighbours
    left_pick = before * ND + send_rows[before, HALO + left_slot]
    right_pick = after * ND + send_rows[after, right_slot]
    source = jnp.where(neighbours < ND, own_pick, jnp.where(neighbours < ND + HALO, left_pick, right_pick)).astype(jnp.int32)
    flat_source = source.reshape(-1)
    active_slots = (jnp.arange(K, dtype=jnp.int32)[None, :] < edge_counts[:, None]).astype(jnp.float32)
    wet_ocean_rows = ocean_mask.astype(jnp.float32)
    weight_per_layer = [(w_edge_in[layer_index], w_edge_out[layer_index], w_node_in[layer_index], w_node_out[layer_index]) for layer_index in range(LAYERS)]

    def one_sample(carry, inputs):
        nodes, edges, node_grad, edge_grad = inputs
        saved_activations = []
        for layer_index in range(LAYERS):
            sources = nodes[flat_source].reshape(NODES, K, D)
            nodes, edges, saved_activation = forward(nodes, edges, sources, active_slots, wet_ocean_rows, weight_per_layer[layer_index])
            saved_activations.append(saved_activation)
        node_gradient = node_grad.astype(jnp.float32)
        edge_gradient = edge_grad.astype(jnp.float32)
        totals = list(carry)
        for layer_index in reversed(range(LAYERS)):
            node_gradient, edge_gradient, source_gradient, layer_gradients = reverse_sweep(saved_activations[layer_index], node_gradient, edge_gradient, active_slots, wet_ocean_rows, weight_per_layer[layer_index])
            node_gradient = node_gradient.at[flat_source].add(source_gradient.reshape(-1, D))
            totals[layer_index] = tuple((total + term for total, term in zip(totals[layer_index], layer_gradients)))
        return (tuple(totals), (node_gradient, edge_gradient.astype(jnp.bfloat16)))
    initial = tuple(((jnp.zeros((3 * D, D), jnp.float32), jnp.zeros((D, D), jnp.float32), jnp.zeros((2 * D, D), jnp.float32), jnp.zeros((D, D), jnp.float32)) for layer_index in range(LAYERS)))
    sums, (grad_nodes, grad_edges) = lax.scan(one_sample, initial, (node_feats, edge_feats, node_cot, edge_cot))
    factor = 1.0 / (SAMPLES * NODES) ** 0.5
    stacked = [jnp.stack([sums[layer_index][kind] for layer_index in range(LAYERS)]) * factor for kind in range(4)]
    return (grad_nodes, grad_edges, stacked[0], stacked[1], stacked[2], stacked[3])
```

```python
import jax
import jax.numpy as jnp
from jax import lax
from jax.experimental import pallas as pl
from jax.experimental.pallas import tpu as pltpu
from jax.sharding import PartitionSpec as P

F32, BF16 = jnp.float32, jnp.bfloat16
D, K, L, ND, H = 512, 8, 2, 64, 16
E = ND * K
BLK = 128
NBLK = E // BLK
PER = BLK // K
CW = D // 2
EPS = 1e-05
NSEM = 192


def nn(a, b):
    return lax.dot_general(a, b, (((1,), (0,)), ((), ())), preferred_element_type=F32)


def nt(a, b):
    return lax.dot_general(a, b, (((1,), (1,)), ((), ())), preferred_element_type=F32)


def tn(a, b):
    return lax.dot_general(a, b, (((0,), (0,)), ((), ())), preferred_element_type=F32)


def iota(shape, axis):
    return lax.broadcasted_iota(jnp.int32, shape, axis)


def row_mean(v):
    return jnp.sum(v, axis=-1, keepdims=True) * (1.0 / D)


def silu_parts(pre):
    sig = 0.5 * jnp.tanh(0.5 * pre) + 0.5
    return (pre * sig).astype(BF16), sig * (1.0 + pre * (1.0 - sig))


def norm_parts(v):
    shifted = v - row_mean(v)
    inverse = lax.rsqrt(row_mean(shifted * shifted) + EPS)
    return shifted * inverse, inverse


def norm_back(normed, inverse, up):
    return inverse * (up - row_mean(up) - normed * row_mean(up * normed))


def device(z, y, x, core):
    return (z * 2 + x % 2) * 2 + core, y * 2 + x // 2


def kernel(
    factor,
    h0, e0, nc, ec, wei_h, weo_h, wni_h, wno_h, nb, send, cnt, oce,
    gn_out, ge_out, oei, oeo, oni, ono,
    wei, weo, wni, wno, wsem, weT, weoT,
    S, ST, SEND, SENDT, live, oc, PQ, pre_s, act, slope, nrm, inv,
    e1, h1, msg, actn, slopen, nrmn, invn, hs, halo, ts, tarr,
    gh, ges, gedge, gpe,
    GX, GY, CX, CY, RA, RB, H1, SA, SB, H2, ZB, AG,
    ssem, rsem,
):
    dp, me = lax.axis_index("dp"), lax.axis_index("mesh")
    core, x_lo, z = dp % 2, (dp // 2) % 2, dp // 4
    y, x_hi = me // 2, me % 2
    x = 2 * x_hi + x_lo

    partner = device(z, y, x, 1 - core)
    right = (device(z, y, (x + 1) % 4, core), device(z, (y + 1) % 4, x, core))
    left = (device(z, y, (x + 3) % 4, core), device(z, (y + 3) % 4, x, core))
    z_peers = [device((z + o) % 8, y, x, core) for o in range(1, 8)]
    mesh_peers = [(dp, (me + o) % 8) for o in range(1, 8)]
    greeted = [partner, right[0], left[0]] + z_peers + mesh_peers
    barrier = pltpu.get_barrier_semaphore()
    for peer in greeted:
        pl.semaphore_signal(barrier, inc=1, device_id=peer, device_id_type=pl.DeviceIdType.MESH)

    loads = {}
    for l in range(L):
        for k, (src, dst) in enumerate(((wei_h, wei), (weo_h, weo), (wni_h, wni), (wno_h, wno))):
            loads[l, k] = pltpu.make_async_copy(src.at[l], dst.at[l], wsem.at[4 * l + k])
            loads[l, k].start()

    copies = []

    def push(src, dst, dev):
        n = len(copies)
        copy = pltpu.make_async_remote_copy(
            src_ref=src, dst_ref=dst, send_sem=ssem.at[n], recv_sem=rsem.at[n],
            device_id=dev, device_id_type=pl.DeviceIdType.MESH,
        )
        copy.start()
        copies.append(copy)
        return copy

    i0, i1 = iota((E, ND), 0), iota((E, ND), 1)
    s_dst = (i0 // K == i1).astype(F32)
    nbf = nb[...].astype(F32)
    spread = jnp.broadcast_to(nbf[:, None, :], (ND, K, K)).reshape(E, K)
    nbcol = jnp.sum(
        jnp.where(iota((E, K), 0) % K == iota((E, K), 1), spread, 0.0), axis=1, keepdims=True
    )
    s_src = (nbcol == iota((E, 128), 1).astype(F32)).astype(F32)
    S[:, 0:128] = s_src.astype(BF16)
    S[:, 128:192] = s_dst.astype(BF16)
    ST[0:128, :] = s_src.T.astype(BF16)
    ST[128:192, :] = (iota((ND, E), 1) // K == iota((ND, E), 0)).astype(F32).astype(BF16)
    countcol = jnp.sum(s_dst * cnt[...].astype(F32), axis=1, keepdims=True)
    live[...] = ((iota((E, 1), 0) % K).astype(F32) < countcol).astype(F32)
    oc[...] = jnp.sum(
        jnp.where(iota((ND, ND), 0) == iota((ND, ND), 1), oce[...].astype(F32), 0.0),
        axis=1, keepdims=True,
    )
    sendf = send[...].astype(F32)
    sendcol = jnp.sum(
        jnp.where(iota((2 * H, 2 * H), 0) == iota((2 * H, 2 * H), 1), sendf, 0.0),
        axis=1, keepdims=True,
    )
    SEND[...] = (sendcol == iota((2 * H, ND), 1).astype(F32)).astype(F32).astype(BF16)
    SENDT[...] = (sendf == iota((ND, 2 * H), 0).astype(F32)).astype(F32).astype(BF16)
    PQ[...] = jnp.zeros_like(PQ)

    pl.semaphore_wait(barrier, len(greeted))

    before, after = (dp, (me + 7) % 8), (dp, (me + 1) % 8)

    def forward(l, h, e):
        hs[l] = nn(SEND[...], h[...]).astype(BF16)
        first = push(hs.at[l, pl.ds(0, H)], halo.at[l, pl.ds(H, H)], before)
        second = push(hs.at[l, pl.ds(H, H)], halo.at[l, pl.ds(0, H)], after)
        loads[l, 0].wait()
        PQ[0:ND, :] = nn(h[...], wei[l, D : 2 * D]).astype(BF16)
        PQ[128:192, :] = nn(h[...], wei[l, 2 * D :]).astype(BF16)
        pre_s[...] = nn(e[...], wei[l, 0:D])
        loads[l, 1].wait()
        weT[l] = wei[l, 0:D].T
        weoT[l] = weo[l].T
        first.wait_recv()
        second.wait_recv()
        PQ[ND : ND + 2 * H, :] = nn(halo[l], wei[l, D : 2 * D]).astype(BF16)
        for b in range(NBLK):
            r = slice(b * BLK, (b + 1) * BLK)
            pre = pre_s[r] + nn(S[r], PQ[...])
            a, sl = silu_parts(pre)
            act[l, r] = a
            slope[l, r] = sl
            n, v = norm_parts(nn(a, weo[l]))
            nrm[l, r] = n
            inv[l, r] = v
            lv = live[r]
            ne = (e[r].astype(F32) + lv * n).astype(BF16)
            if l + 1 < L:
                e1[r] = ne
            m = jnp.sum((lv * ne.astype(F32)).reshape(PER, K, D), axis=1)
            msg[l, b * PER : (b + 1) * PER] = m.astype(BF16)
        loads[l, 2].wait()
        loads[l, 3].wait()
        pre = nn(h[...], wni[l, 0:D]) + nn(msg[l], wni[l, D:])
        a, sl = silu_parts(pre)
        actn[l] = a
        slopen[l] = sl
        n, v = norm_parts(nn(a, wno[l]))
        nrmn[l] = n
        invn[l] = v
        if l + 1 < L:
            h1[...] = (h[...].astype(F32) + oc[...] * n).astype(BF16)

    forward(0, h0, e0)
    forward(1, h1, e1)

    def store_unit(l, kind, unit, val):
        per, base = ((3, 0), (1, 3), (2, 4), (1, 6))[kind]
        for c in range(D // 16):
            at = unit * (D // 16) + c
            d, j = at // per, base + at % per
            dcore, dxl, dz = d % 2, (d // 2) % 2, d // 4
            dy, dx = j // 2, 2 * (j % 2) + dxl
            piece = val[16 * c : 16 * c + 16].astype(BF16)
            GX[l, dcore, dx, dy, dz] = piece[:, 0:CW]
            GY[l, dcore, dy, dx, dz] = piece[:, CW:]

    for l in range(L):
        for dcore in range(2):
            for dx in (2, 3):
                GX[l, dcore, dx, 3] = jnp.zeros((8, 16, CW), BF16)
                GY[l, dcore, 3, dx] = jnp.zeros((8, 16, CW), BF16)

    gh[...] = nc[...].astype(F32)
    ges[...] = ec[...].astype(F32)

    def node_back(l, h):
        gout = norm_back(nrmn[l], invn[l], oc[...] * gh[...]).astype(BF16)
        gpre = (nt(gout, wno[l]) * slopen[l]).astype(BF16)
        gin = nt(gpre, wni[l])
        gh[...] = gh[...] + gin[:, 0:D]
        return gout, gpre, gin[:, D:]

    def edge_back(l, gm, e):
        for b in range(NBLK):
            r = slice(b * BLK, (b + 1) * BLK)
            lv = live[r]
            part = gm[b * PER : (b + 1) * PER]
            part = jnp.broadcast_to(part[:, None, :], (PER, K, D)).reshape(BLK, D)
            ge2 = ges[r] + lv * part
            g = norm_back(nrm[l, r], inv[l, r], lv * ge2).astype(BF16)
            gedge[r] = g
            gp = (nn(g, weoT[l]) * slope[l, r]).astype(BF16)
            gpe[r] = gp
            new = ge2 + nn(gp, weT[l])
            if l:
                ges[r] = new
            else:
                ge_out[r] = new.astype(BF16)

    def finish_layer(l, h, e, gout, gpre):
        td = nn(ST[...], gpe[...])
        ts[l] = td[ND : ND + 2 * H].astype(BF16)
        first = push(ts.at[l, pl.ds(0, H)], tarr.at[l, pl.ds(H, H)], before)
        second = push(ts.at[l, pl.ds(H, H)], tarr.at[l, pl.ds(0, H)], after)
        dst = td[128:192].astype(BF16)
        ht = h[...].T
        store_unit(l, 1, 0, tn(act[l], gedge[...]))
        store_unit(l, 0, 0, tn(e[...], gpe[...]))
        store_unit(l, 0, 2, nn(ht, dst))
        store_unit(l, 2, 0, nn(ht, gpre))
        store_unit(l, 2, 1, tn(msg[l], gpre))
        store_unit(l, 3, 0, tn(actn[l], gout))
        first.wait_recv()
        second.wait_recv()
        src = (td[0:ND] + nn(SENDT[...], tarr[l])).astype(BF16)
        pre_s[0:ND] = nt(src, wei[l, D : 2 * D]) + nt(dst, wei[l, 2 * D :])
        into = gh if l else gn_out

        @pl.loop(0, ND // 8)
        def _(i):
            r = pl.ds(pl.multiple_of(8 * i, 8), 8)
            into[r] = gh[r] + pre_s[r]
        store_unit(l, 0, 1, nn(ht, src))

    G, C = (GX, GY), (CX, CY)
    pos = ((x, y), (y, x))

    def swap(l):
        return [push(G[c].at[l, 1 - core], C[c].at[l], partner) for c in range(2)]

    def ring_open(c, axis, half, at, ra, rb, ready):
        a = pos[c][axis]
        rdev, ldev = right[(c + axis) % 2], left[(c + axis) % 2]
        r, o, q = (a + 1) % 4, (a + 2) % 4, (a + 3) % 4
        lo, hi = pl.ds(0, half), pl.ds(half, half)
        ready(o)
        m1r = push(at(o).at[lo], ra.at[0], rdev)
        m1l = push(at(o).at[hi], ra.at[1], ldev)
        ready(r)
        m2r = push(at(r).at[hi], rb.at[0, hi], rdev)
        ready(q)
        m2l = push(at(q).at[lo], rb.at[1, lo], ldev)
        ready(a)

        def relay():
            m1r.wait_recv()
            for i in range(half):
                at(r)[i] = at(r)[i] + ra[0, i]
            m3r = push(at(r).at[lo], rb.at[0, lo], rdev)
            m1l.wait_recv()
            for i in range(half):
                at(q)[half + i] = at(q)[half + i] + ra[1, i]
            m3l = push(at(q).at[hi], rb.at[1, hi], ldev)
            return m3r, m3l

        def close(ends, out):
            for m in (m2r, m2l) + ends:
                m.wait_recv()
            for i in range(2 * half):
                total = at(a)[i].astype(F32) + rb[0, i].astype(F32) + rb[1, i].astype(F32)
                out[i] = total.astype(BF16)

        return relay, close

    def stage1(l, c):
        def at(i):
            return G[c].at[l, core, i]

        def ready(i):
            for k in range(4):
                at(i)[k] = at(i)[k] + C[c][l, i, k]

        return ring_open(c, 0, 2, at, RA.at[l, c], RB.at[l, c], ready)

    def stage2(l, c):
        def at(i):
            return H1.at[l, c, i]

        return ring_open(c, 1, 4, at, SA.at[l, c], SB.at[l, c], lambda i: None)

    def stage3(l, c):
        return [
            push(H2.at[l, c, (z + o) % 8], ZB.at[l, c, o], z_peers[o - 1]) for o in range(1, 8)
        ]

    def stage3_end(l, c, pushed):
        for m in pushed:
            m.wait_recv()
        total = H2[l, c, z].astype(F32)
        for o in range(1, 8):
            total = total + ZB[l, c, o].astype(F32)
        AG[l, me, :, c * CW : (c + 1) * CW] = total.astype(BF16)

    def gather(l):
        return [push(AG.at[l, me], AG.at[l, me], mesh_peers[o - 1]) for o in range(1, 8)]

    def write(l, pushed):
        for m in pushed:
            m.wait_recv()
        for j in range(7):
            ref, row = ((oei, j), (oeo, 0), (oni, j - 4), (ono, 0))[0 if j < 3 else (1 if j == 3 else (2 if j < 6 else 3))]
            ref[l, 16 * row : 16 * row + 16, :] = AG[l, j].astype(F32) * factor

    gout, gpre, gm = node_back(1, h1)
    edge_back(1, gm, e1)
    finish_layer(1, h1, e1, gout, gpre)
    swapped1 = swap(1)
    gout, gpre, gm = node_back(0, h0)
    for m in swapped1:
        m.wait_recv()
    first1 = [stage1(1, c) for c in range(2)]
    edge_back(0, gm, e0)
    ends1 = [relay() for relay, _ in first1]
    finish_layer(0, h0, e0, gout, gpre)
    swapped0 = swap(0)

    def close(l, opened, ends, out):
        for c in range(2):
            opened[c][1](ends[c], out.at[l, c])

    close(1, first1, ends1, H1)
    second1 = [stage2(1, c) for c in range(2)]
    for m in swapped0:
        m.wait_recv()
    first0 = [stage1(0, c) for c in range(2)]
    ends1 = [relay() for relay, _ in second1]
    ends0 = [relay() for relay, _ in first0]
    close(1, second1, ends1, H2)
    third1 = [stage3(1, c) for c in range(2)]
    close(0, first0, ends0, H1)
    second0 = [stage2(0, c) for c in range(2)]
    for c in range(2):
        stage3_end(1, c, third1[c])
    last1 = gather(1)
    ends0 = [relay() for relay, _ in second0]
    close(0, second0, ends0, H2)
    third0 = [stage3(0, c) for c in range(2)]
    write(1, last1)
    for c in range(2):
        stage3_end(0, c, third0[c])
    write(0, gather(0))
    for copy in copies:
        copy.wait_send()


def body(
    node_feats, edge_feats, node_cot, edge_cot, w_edge_in, w_edge_out, w_node_in, w_node_out,
    neighbours, send_rows, edge_counts, ocean_mask,
):
    samples, nodes, features = node_feats.shape
    total_rows = samples * lax.axis_size("dp") * nodes * lax.axis_size("mesh")
    factor = 1.0 / total_rows**0.5
    vmem = pl.BlockSpec(memory_space=pltpu.VMEM)
    hbm = pl.BlockSpec(memory_space=pl.ANY)

    def buf(dtype, *shape):
        return pltpu.VMEM(shape, dtype)

    scratch = [
        buf(BF16, L, 3 * D, D), buf(BF16, L, D, D), buf(BF16, L, 2 * D, D), buf(BF16, L, D, D),
        pltpu.SemaphoreType.DMA((4 * L,)),
        buf(BF16, L, D, D), buf(BF16, L, D, D),
        buf(BF16, E, 192), buf(BF16, 192, E), buf(BF16, 2 * H, ND), buf(BF16, ND, 2 * H),
        buf(F32, E, 1), buf(F32, ND, 1), buf(BF16, 192, D), buf(F32, E, D),
        buf(BF16, L, E, D), buf(F32, L, E, D), buf(F32, L, E, D), buf(F32, L, E, 1),
        buf(BF16, E, D), buf(BF16, ND, D), buf(BF16, L, ND, D),
        buf(BF16, L, ND, D), buf(F32, L, ND, D), buf(F32, L, ND, D), buf(F32, L, ND, 1),
        buf(BF16, L, 2 * H, D), buf(BF16, L, 2 * H, D),
        buf(BF16, L, 2 * H, D), buf(BF16, L, 2 * H, D),
        buf(F32, ND, D), buf(F32, E, D), buf(BF16, E, D), buf(BF16, E, D),
        buf(BF16, L, 2, 4, 4, 8, 16, CW), buf(BF16, L, 2, 4, 4, 8, 16, CW),
        buf(BF16, L, 4, 4, 8, 16, CW), buf(BF16, L, 4, 4, 8, 16, CW),
        buf(BF16, L, 2, 2, 2, 8, 16, CW), buf(BF16, L, 2, 2, 4, 8, 16, CW),
        buf(BF16, L, 2, 4, 8, 16, CW),
        buf(BF16, L, 2, 2, 4, 16, CW), buf(BF16, L, 2, 2, 8, 16, CW),
        buf(BF16, L, 2, 8, 16, CW), buf(BF16, L, 2, 8, 16, CW), buf(BF16, L, 8, 16, D),
        pltpu.SemaphoreType.DMA((NSEM,)), pltpu.SemaphoreType.DMA((NSEM,)),
    ]

    def run(*refs):
        return kernel(factor, *refs)

    outs = pl.pallas_call(
        run,
        out_shape=(
            jax.ShapeDtypeStruct((ND, D), F32),
            jax.ShapeDtypeStruct((E, D), BF16),
            jax.ShapeDtypeStruct((L, 48, D), F32),
            jax.ShapeDtypeStruct((L, 16, D), F32),
            jax.ShapeDtypeStruct((L, 32, D), F32),
            jax.ShapeDtypeStruct((L, 16, D), F32),
        ),
        in_specs=[vmem] * 4 + [hbm] * 4 + [vmem] * 4,
        out_specs=(vmem,) * 6,
        scratch_shapes=scratch,
        compiler_params=pltpu.CompilerParams(
            collective_id=0, has_side_effects=True, vmem_limit_bytes=60 << 20
        ),
    )(
        node_feats.reshape(ND, D), edge_feats.reshape(E, D),
        node_cot.reshape(ND, D), edge_cot.reshape(E, D),
        w_edge_in, w_edge_out, w_node_in, w_node_out,
        neighbours, send_rows, edge_counts.reshape(1, ND), ocean_mask.reshape(1, ND),
    )
    return (outs[0].reshape(samples, nodes, D), outs[1].reshape(samples, nodes, K, D)) + tuple(outs[2:])


def solution(mesh):
    rows, edges = P("dp", "mesh", None), P("dp", "mesh", None, None)
    weight = P(None, "dp", None)
    return jax.shard_map(
        body,
        mesh=mesh,
        in_specs=(
            rows, edges, rows, edges, P(), P(), P(), P(),
            P("mesh", None), P("mesh", None), P("mesh"), P("mesh"),
        ),
        out_specs=(rows, edges, weight, weight, weight, weight),
        check_vma=False,
    )
```

```python
import jax
import jax.numpy as jnp
from jax import lax
from jax.experimental import pallas as pl
from jax.experimental.pallas import tpu as pltpu
from jax.sharding import PartitionSpec as P

F32, BF16 = jnp.float32, jnp.bfloat16
D, K, L, ND, H = 512, 8, 2, 64, 16
E = ND * K
BLK = 128
NBLK = E // BLK
PER = BLK // K
EPS = 1e-05
NSEM = 144
GROUPS = (((3, 6), (0, 1, 2), (4, 5)), ((0, 1, 2), (3, 6), (4, 5)))


def nn(a, b):
    return lax.dot_general(a, b, (((1,), (0,)), ((), ())), preferred_element_type=F32)


def nt(a, b):
    return lax.dot_general(a, b, (((1,), (1,)), ((), ())), preferred_element_type=F32)


def tn(a, b):
    return lax.dot_general(a, b, (((0,), (0,)), ((), ())), preferred_element_type=F32)


def iota(shape, axis):
    return lax.broadcasted_iota(jnp.int32, shape, axis)


def row_mean(v):
    return jnp.sum(v, axis=-1, keepdims=True) * (1.0 / D)


def silu_parts(pre):
    sig = 0.5 * jnp.tanh(0.5 * pre) + 0.5
    return (pre * sig).astype(BF16), sig * (1.0 + pre * (1.0 - sig))


def norm_parts(v):
    shifted = v - row_mean(v)
    inverse = lax.rsqrt(row_mean(shifted * shifted) + EPS)
    return shifted * inverse, inverse


def norm_back(normed, inverse, up):
    return inverse * (up - row_mean(up) - normed * row_mean(up * normed))


def device(z, y, x, core):
    return (z * 2 + x % 2) * 2 + core, y * 2 + x // 2


def kernel(
    h0, e0, nc, ec, wei_h, weo_h, wni_h, wno_h, nb, send, cnt, oce,
    gn_out, ge_out, wg_out,
    wei, weo, wni, wno, wsem, weT, weoT,
    S, ST, SEND, SENDT, live, oc, PQ, pre_s, act, slope, nrm, inv,
    e1, h1, msg, actn, slopen, nrmn, invn, hs, halo, ts, tarr,
    gh, ges, gedge, gpe,
    AG, ssem, rsem, *rest,
):
    dp, me = lax.axis_index("dp"), lax.axis_index("mesh")
    core, x_lo, z = dp % 2, (dp // 2) % 2, dp // 4
    y, x_hi = me // 2, me % 2
    x = 2 * x_hi + x_lo

    partner = device(z, y, x, 1 - core)
    right = (device(z, y, (x + 1) % 4, core), device(z, (y + 1) % 4, x, core), device((z + 1) % 8, y, x, core))
    left = (device(z, y, (x + 3) % 4, core), device(z, (y + 3) % 4, x, core), device((z + 7) % 8, y, x, core))
    z_peers = [device((z + o) % 8, y, x, core) for o in range(1, 8)]
    plane = {
        (ox, oy): device(z, (y + oy) % 4, (x + ox) % 4, core)
        for ox in range(4) for oy in range(4) if ox or oy
    }
    mesh_peers = [(dp, (me + o) % 8) for o in range(1, 8)]
    greeted = [partner] + z_peers + list(plane.values())
    barrier = pltpu.get_barrier_semaphore()
    for peer in greeted:
        pl.semaphore_signal(barrier, inc=1, device_id=peer, device_id_type=pl.DeviceIdType.MESH)

    loads = {}
    for l in range(L):
        for k, (src, dst) in enumerate(((wei_h, wei), (weo_h, weo), (wni_h, wni), (wno_h, wno))):
            loads[l, k] = pltpu.make_async_copy(src.at[l], dst.at[l], wsem.at[4 * l + k])
            loads[l, k].start()

    copies = []

    def push(src, dst, dev):
        n = len(copies)
        copy = pltpu.make_async_remote_copy(
            src_ref=src, dst_ref=dst, send_sem=ssem.at[n], recv_sem=rsem.at[n],
            device_id=dev, device_id_type=pl.DeviceIdType.MESH,
        )
        copy.start()
        copies.append(copy)
        return copy

    i0, i1 = iota((E, ND), 0), iota((E, ND), 1)
    s_dst = (i0 // K == i1).astype(F32)
    spread = nt(s_dst.astype(BF16), nb[...].astype(F32).astype(BF16))
    nbcol = jnp.sum(
        jnp.where(iota((E, K), 0) % K == iota((E, K), 1), spread, 0.0), axis=1, keepdims=True
    )
    s_src = (nbcol == iota((E, 128), 1).astype(F32)).astype(F32)
    S[:, 0:128] = s_src.astype(BF16)
    S[:, 128:192] = s_dst.astype(BF16)
    ST[0:128, :] = s_src.T.astype(BF16)
    ST[128:192, :] = (iota((ND, E), 1) // K == iota((ND, E), 0)).astype(F32).astype(BF16)
    countcol = jnp.sum(s_dst * cnt[...].astype(F32), axis=1, keepdims=True)
    live[...] = ((iota((E, 1), 0) % K).astype(F32) < countcol).astype(F32)
    oc[...] = jnp.sum(
        jnp.where(iota((ND, ND), 0) == iota((ND, ND), 1), oce[...].astype(F32), 0.0),
        axis=1, keepdims=True,
    )
    sendf = send[...].astype(F32)
    sendcol = jnp.sum(
        jnp.where(iota((2 * H, 2 * H), 0) == iota((2 * H, 2 * H), 1), sendf, 0.0),
        axis=1, keepdims=True,
    )
    SEND[...] = (sendcol == iota((2 * H, ND), 1).astype(F32)).astype(F32).astype(BF16)
    SENDT[...] = (sendf == iota((ND, 2 * H), 0).astype(F32)).astype(F32).astype(BF16)
    PQ[...] = jnp.zeros_like(PQ)

    before, after = (dp, (me + 7) % 8), (dp, (me + 1) % 8)

    def forward(l, h, e):
        hs[l] = nn(SEND[...], h[...]).astype(BF16)

        def local():
            loads[l, 0].wait()
            PQ[0:ND, :] = nn(h[...], wei[l, D : 2 * D]).astype(BF16)
            PQ[128:192, :] = nn(h[...], wei[l, 2 * D :]).astype(BF16)
            pre_s[...] = nn(e[...], wei[l, 0:D])
            loads[l, 1].wait()
            weT[l] = wei[l, 0:D].T
            weoT[l] = weo[l].T

        if l == 0:
            local()
            pl.semaphore_wait(barrier, len(greeted))
        first = push(hs.at[l, pl.ds(0, H)], halo.at[l, pl.ds(H, H)], before)
        second = push(hs.at[l, pl.ds(H, H)], halo.at[l, pl.ds(0, H)], after)
        if l:
            local()
        first.wait_recv()
        second.wait_recv()
        PQ[ND : ND + 2 * H, :] = nn(halo[l], wei[l, D : 2 * D]).astype(BF16)
        for b in range(NBLK):
            r = slice(b * BLK, (b + 1) * BLK)
            pre = pre_s[r] + nn(S[r], PQ[...])
            a, sl = silu_parts(pre)
            act[l, r] = a
            slope[l, r] = sl
            n, v = norm_parts(nn(a, weo[l]))
            nrm[l, r] = n
            inv[l, r] = v
            lv = live[r]
            ne = (e[r].astype(F32) + lv * n).astype(BF16)
            if l + 1 < L:
                e1[r] = ne
            m = jnp.sum((lv * ne.astype(F32)).reshape(PER, K, D), axis=1)
            msg[l, b * PER : (b + 1) * PER] = m.astype(BF16)
        loads[l, 2].wait()
        loads[l, 3].wait()
        pre = nn(h[...], wni[l, 0:D]) + nn(msg[l], wni[l, D:])
        a, sl = silu_parts(pre)
        actn[l] = a
        slopen[l] = sl
        n, v = norm_parts(nn(a, wno[l]))
        nrmn[l] = n
        invn[l] = v
        if l + 1 < L:
            h1[...] = (h[...].astype(F32) + oc[...] * n).astype(BF16)

    forward(0, h0, e0)
    forward(1, h1, e1)

    bufs = iter(rest)
    G, C, RA, RB, T1, SB, T2, ZB = {}, {}, {}, {}, {}, {}, {}, {}
    for l in range(L):
        for c in range(3):
            names = (G, C, RA, RB, T1, SB, T2, ZB) if c < 2 else (G, C, RA, RB, T1, SB)
            for name in names:
                name[l, c] = next(bufs)

    def store_unit(l, kind, unit, val):
        per, base = ((3, 0), (1, 3), (2, 4), (1, 6))[kind]
        val = val.astype(BF16)
        for n in range(D // 16):
            at = unit * (D // 16) + n
            d, j = at // per, base + at % per
            dcore, dxl, dz = d % 2, (d // 2) % 2, d // 4
            c = [j in GROUPS[l][k] for k in range(3)].index(True)
            g = GROUPS[l][c].index(j)
            for dxh in range(2):
                for dy in range(4):
                    dx = 2 * dxh + dxl
                    place = ((dx, dy, dz), (dy, dx, dz), (dz, dx, dy))[c]
                    row = 16 * n + 8 * dxh
                    G[l, c][(dcore,) + place + (g,)] = val[row : row + 8, 128 * dy : 128 * dy + 128]

    gh[...] = nc[...].astype(F32)
    ges[...] = ec[...].astype(F32)

    def node_back(l, h):
        gout = norm_back(nrmn[l], invn[l], oc[...] * gh[...]).astype(BF16)
        gpre = (nt(gout, wno[l]) * slopen[l]).astype(BF16)
        gin = nt(gpre, wni[l])
        gh[...] = gh[...] + gin[:, 0:D]
        store_unit(l, 2, 0, tn(h[...], gpre))
        store_unit(l, 2, 1, tn(msg[l], gpre))
        store_unit(l, 3, 0, tn(actn[l], gout))
        return gin[:, D:]

    def edge_back(l, gm, e):
        for b in range(NBLK):
            r = slice(b * BLK, (b + 1) * BLK)
            lv = live[r]
            part = gm[b * PER : (b + 1) * PER]
            part = jnp.broadcast_to(part[:, None, :], (PER, K, D)).reshape(BLK, D)
            ge2 = ges[r] + lv * part
            g = norm_back(nrm[l, r], inv[l, r], lv * ge2).astype(BF16)
            gedge[r] = g
            gp = (nn(g, weoT[l]) * slope[l, r]).astype(BF16)
            gpe[r] = gp
            new = ge2 + nn(gp, weT[l])
            if l:
                ges[r] = new
            else:
                ge_out[r] = new.astype(BF16)

    def finish_layer(l, h, e):
        td = nn(ST[...], gpe[...])
        ts[l] = td[ND : ND + 2 * H].astype(BF16)
        first = push(ts.at[l, pl.ds(0, H)], tarr.at[l, pl.ds(H, H)], before)
        second = push(ts.at[l, pl.ds(H, H)], tarr.at[l, pl.ds(0, H)], after)
        dst = td[128:192].astype(BF16)
        ht = h[...].T
        store_unit(l, 1, 0, tn(act[l], gedge[...]))
        store_unit(l, 0, 0, tn(e[...], gpe[...]))
        store_unit(l, 0, 2, nn(ht, dst))
        first.wait_recv()
        second.wait_recv()
        src = (td[0:ND] + nn(SENDT[...], tarr[l])).astype(BF16)
        pre_s[0:ND] = nt(src, wei[l, D : 2 * D]) + nt(dst, wei[l, 2 * D :])
        into = gh if l else gn_out

        @pl.loop(0, ND // 8)
        def _(i):
            r = pl.ds(pl.multiple_of(8 * i, 8), 8)
            into[r] = gh[r] + pre_s[r]
        store_unit(l, 0, 1, nn(ht, src))

    pos = ((x, y), (y, x))

    def swap(l, c):
        return push(G[l, c].at[1 - core], C[l, c], partner)

    def settle(l, c, i):
        ref, got = G[l, c].at[core, i], C[l, c].at[i]
        for k in range(4):
            ref[k] = ref[k] + got[k]

    def ring4(l, c, swapped):
        swapped.wait_recv()
        ref, ra, rb = G[l, c], RA[l, c], RB[l, c]
        a = pos[c][0]
        r, o, q = (a + 1) % 4, (a + 2) % 4, (a + 3) % 4
        lo, hi = pl.ds(0, 2), pl.ds(2, 2)
        settle(l, c, o)
        m1r = push(ref.at[core, o, lo], ra.at[0], right[c])
        m1l = push(ref.at[core, o, hi], ra.at[1], left[c])
        settle(l, c, r)
        m2r = push(ref.at[core, r, hi], rb.at[0, hi], right[c])
        settle(l, c, q)
        m2l = push(ref.at[core, q, lo], rb.at[1, lo], left[c])
        settle(l, c, a)

        def relay():
            m1r.wait_recv()
            for i in range(2):
                ref[core, r, i] = ref[core, r, i] + ra[0, i]
            m3r = push(ref.at[core, r, lo], rb.at[0, lo], right[c])
            m1l.wait_recv()
            for i in range(2):
                ref[core, q, 2 + i] = ref[core, q, 2 + i] + ra[1, i]
            m3l = push(ref.at[core, q, hi], rb.at[1, hi], left[c])

            def close():
                for m in (m2r, m2l, m3r, m3l):
                    m.wait_recv()
                for i in range(4):
                    total = ref[core, a, i].astype(F32) + rb[0, i].astype(F32) + rb[1, i].astype(F32)
                    T1[l, c][i] = total.astype(BF16)

            return close

        return relay

    def across(l, c):
        b = pos[c][1]
        t, s = T1[l, c], SB[l, c]
        peer = [plane[(0, o) if c == 0 else (o, 0)] for o in range(1, 4)]
        sent = [push(t.at[(b + o) % 4], s.at[o], peer[o - 1]) for o in range(1, 4)]

        def close():
            for m in sent:
                m.wait_recv()
            total = t[b].astype(F32)
            for o in range(1, 4):
                total = total + s[o].astype(F32)
            T2[l, c][...] = total.astype(BF16)

        return close

    def keep(l, c, total):
        for g, j in enumerate(GROUPS[l][c]):
            AG[l, me, j] = total[g].astype(BF16)

    def along(l, c):
        t, s = T2[l, c], ZB[l, c]
        sent = [push(t.at[(z + o) % 8], s.at[o], z_peers[o - 1]) for o in range(1, 8)]

        def close():
            for m in sent:
                m.wait_recv()
            total = t[z].astype(F32)
            for o in range(1, 8):
                total = total + s[o].astype(F32)
            keep(l, c, total)

        return close

    def ring8(l, swapped):
        swapped.wait_recv()
        ref, first, full = G[l, 2], RA[l, 2], RB[l, 2]
        lo, hi = pl.ds(0, 2), pl.ds(2, 2)
        far = (z + 4) % 8
        settle(l, 2, far)
        got = [
            push(ref.at[core, far, lo], first.at[0], right[2]),
            push(ref.at[core, far, hi], first.at[1], left[2]),
        ]
        for o in (3, 5, 2, 6, 1, 7, 0):
            settle(l, 2, (z + o) % 8)

        def step(n):
            for way in range(2):
                got[way].wait_recv()
                at = (z + (4 - n if way == 0 else 4 + n)) % 8
                if n == 1:
                    for i in range(2):
                        ref[core, at, 2 * way + i] = ref[core, at, 2 * way + i] + first[way, i]
                else:
                    for i in range(4):
                        ref[core, at, i] = ref[core, at, i] + full[way, n - 2, i]
                got[way] = push(
                    ref.at[core, at], full.at[way, n - 1], (right, left)[way][2]
                )

        def close():
            for way in range(2):
                got[way].wait_recv()
            for i in range(4):
                total = ref[core, z, i].astype(F32) + full[0, 2, i].astype(F32) + full[1, 2, i].astype(F32)
                T1[l, 2][i] = total.astype(BF16)

        return step, close

    def spread_plane(l):
        t, s = T1[l, 2], SB[l, 2]
        sent = [
            push(t.at[(x + ox) % 4, (y + oy) % 4], s.at[ox, oy], dev) for (ox, oy), dev in plane.items()
        ]

        def close():
            for m in sent:
                m.wait_recv()
            total = t[x, y].astype(F32)
            for ox, oy in plane:
                total = total + s[ox, oy].astype(F32)
            keep(l, 2, total)

        return close

    def gather(l):
        return [push(AG.at[l, me], AG.at[l, me], peer) for peer in mesh_peers]

    def write(l, pushed):
        for m in pushed:
            m.wait_recv()
        wg_out[l] = AG[l]

    both = lambda fn, l: [fn(l, c) for c in range(2)]
    run = lambda fns: [fn() for fn in fns]

    gm = node_back(1, h1)
    swz1 = swap(1, 2)
    edge_back(1, gm, e1)
    finish_layer(1, h1, e1)
    sw1 = both(swap, 1)
    z1, z1_close = ring8(1, swz1)
    gm = node_back(0, h0)
    swz0 = swap(0, 2)
    z1(1)
    xy1 = [ring4(1, c, sw1[c]) for c in range(2)]
    edge_back(0, gm, e0)
    z1(2)
    xy1 = run(xy1)
    z0, z0_close = ring8(0, swz0)
    finish_layer(0, h0, e0)
    sw0 = both(swap, 0)
    z1(3)
    z0(1)
    run(xy1)
    xy1 = both(across, 1)
    xy0 = [ring4(0, c, sw0[c]) for c in range(2)]
    z1_close()
    z1_end = spread_plane(1)
    z0(2)
    run(xy1)
    xy1 = both(along, 1)
    xy0 = run(xy0)
    z0(3)
    z1_end()
    run(xy1)
    last1 = gather(1)
    z0_close()
    z0_end = spread_plane(0)
    run(xy0)
    xy0 = both(across, 0)
    z0_end()
    run(xy0)
    xy0 = both(along, 0)
    write(1, last1)
    run(xy0)
    write(0, gather(0))
    for copy in copies:
        copy.wait_send()


def body(
    node_feats, edge_feats, node_cot, edge_cot, w_edge_in, w_edge_out, w_node_in, w_node_out,
    neighbours, send_rows, edge_counts, ocean_mask,
):
    samples, nodes, features = node_feats.shape
    total_rows = samples * lax.axis_size("dp") * nodes * lax.axis_size("mesh")
    factor = 1.0 / total_rows**0.5
    vmem = pl.BlockSpec(memory_space=pltpu.VMEM)
    hbm = pl.BlockSpec(memory_space=pl.ANY)

    def buf(dtype, *shape):
        return pltpu.VMEM(shape, dtype)

    scratch = [
        buf(BF16, L, 3 * D, D), buf(BF16, L, D, D), buf(BF16, L, 2 * D, D), buf(BF16, L, D, D),
        pltpu.SemaphoreType.DMA((4 * L,)),
        buf(BF16, L, D, D), buf(BF16, L, D, D),
        buf(BF16, E, 192), buf(BF16, 192, E), buf(BF16, 2 * H, ND), buf(BF16, ND, 2 * H),
        buf(F32, E, 1), buf(F32, ND, 1), buf(BF16, 192, D), buf(F32, E, D),
        buf(BF16, L, E, D), buf(F32, L, E, D), buf(F32, L, E, D), buf(F32, L, E, 1),
        buf(BF16, E, D), buf(BF16, ND, D), buf(BF16, L, ND, D),
        buf(BF16, L, ND, D), buf(F32, L, ND, D), buf(F32, L, ND, D), buf(F32, L, ND, 1),
        buf(BF16, L, 2 * H, D), buf(BF16, L, 2 * H, D),
        buf(BF16, L, 2 * H, D), buf(BF16, L, 2 * H, D),
        buf(F32, ND, D), buf(F32, E, D), buf(BF16, E, D), buf(BF16, E, D),
        buf(BF16, L, 8, 7, 8, 128),
        pltpu.SemaphoreType.DMA((NSEM,)), pltpu.SemaphoreType.DMA((NSEM,)),
    ]
    for l in range(L):
        for c in range(3):
            tile = (len(GROUPS[l][c]), 8, 128)
            if c < 2:
                shapes = (
                    (2, 4, 4, 8), (4, 4, 8), (2, 2, 8), (2, 4, 8), (4, 8), (4, 8), (8,), (8,),
                )
            else:
                shapes = ((2, 8, 4, 4), (8, 4, 4), (2, 2, 4), (2, 3, 4, 4), (4, 4), (4, 4))
            scratch += [buf(BF16, *(shape + tile)) for shape in shapes]

    done = pl.pallas_call(
        kernel,
        out_shape=(
            jax.ShapeDtypeStruct((ND, D), F32),
            jax.ShapeDtypeStruct((E, D), BF16),
            jax.ShapeDtypeStruct((L, 8, 7, 8, 128), BF16),
        ),
        in_specs=[vmem] * 4 + [hbm] * 4 + [vmem] * 4,
        out_specs=(vmem,) * 3,
        scratch_shapes=scratch,
        compiler_params=pltpu.CompilerParams(
            collective_id=0, has_side_effects=True, vmem_limit_bytes=60 << 20
        ),
    )(
        node_feats.reshape(ND, D), edge_feats.reshape(E, D),
        node_cot.reshape(ND, D), edge_cot.reshape(E, D),
        w_edge_in, w_edge_out, w_node_in, w_node_out,
        neighbours.T, send_rows, edge_counts.reshape(1, ND), ocean_mask.reshape(1, ND),
    )

    def finish(gn, ge, wg, gn_out, ge_out, oei, oeo, oni, ono):
        gn_out[...] = gn[...]
        ge_out[...] = ge[...]
        for l in range(L):
            for j in range(7):
                ref, row = ((oei, j), (oei, j), (oei, j), (oeo, 0), (oni, 0), (oni, 1), (ono, 0))[j]
                for m in range(8):
                    r, q = 16 * row + 8 * (m % 2), 128 * (m // 2)
                    ref[l, r : r + 8, q : q + 128] = wg[l, m, j].astype(F32) * factor

    outs = pl.pallas_call(
        finish,
        out_shape=(
            jax.ShapeDtypeStruct((ND, D), F32),
            jax.ShapeDtypeStruct((E, D), BF16),
            jax.ShapeDtypeStruct((L, 48, D), F32),
            jax.ShapeDtypeStruct((L, 16, D), F32),
            jax.ShapeDtypeStruct((L, 32, D), F32),
            jax.ShapeDtypeStruct((L, 16, D), F32),
        ),
        in_specs=[vmem] * 3,
        out_specs=(vmem,) * 6,
    )(*done)
    return (outs[0].reshape(samples, nodes, D), outs[1].reshape(samples, nodes, K, D)) + tuple(outs[2:])


def solution(mesh):
    rows, edges = P("dp", "mesh", None), P("dp", "mesh", None, None)
    weight = P(None, "dp", None)
    return jax.shard_map(
        body,
        mesh=mesh,
        in_specs=(
            rows, edges, rows, edges, P(), P(), P(), P(),
            P("mesh", None), P("mesh", None), P("mesh"), P("mesh"),
        ),
        out_specs=(rows, edges, weight, weight, weight, weight),
        check_vma=False,
    )
```

```python
import jax
import jax.numpy as jnp
from jax import lax
from jax.experimental import pallas as pl
from jax.experimental.pallas import tpu as pltpu
from jax.sharding import PartitionSpec as P

F32, BF16 = jnp.float32, jnp.bfloat16
D, K, L, ND, H = 512, 8, 2, 64, 16
E = ND * K
BLK = 256
NBLK = E // BLK
PER = BLK // K
EPS = 1e-05
NSEM = 144
GROUPS = (((0, 3), (1, 2), (4, 5, 6)),) * L


def nn(a, b):
    return lax.dot_general(a, b, (((1,), (0,)), ((), ())), preferred_element_type=F32)


def nt(a, b):
    return lax.dot_general(a, b, (((1,), (1,)), ((), ())), preferred_element_type=F32)


def tn(a, b):
    return lax.dot_general(a, b, (((0,), (0,)), ((), ())), preferred_element_type=F32)


def iota(shape, axis):
    return lax.broadcasted_iota(jnp.int32, shape, axis)


def row_mean(v):
    return jnp.sum(v, axis=-1, keepdims=True) * (1.0 / D)


def silu_parts(pre):
    sig = 0.5 * jnp.tanh(0.5 * pre) + 0.5
    return (pre * sig).astype(BF16), sig * (1.0 + pre * (1.0 - sig))


def norm_parts(v):
    shifted = v - row_mean(v)
    inverse = lax.rsqrt(row_mean(shifted * shifted) + EPS)
    return shifted * inverse, inverse


def norm_back(normed, inverse, up):
    return inverse * (up - row_mean(up) - normed * row_mean(up * normed))


def device(z, y, x, core):
    return (z * 2 + x % 2) * 2 + core, y * 2 + x // 2


def kernel(
    h0, e0, nc, ec, wei_h, weo_h, wni_h, wno_h, nb, send, cnt, oce,
    gn_out, ge_out, wg_out,
    wei, weo, wni, wno, wsem,
    S, ST, SEND, SENDT, live, oc, PQ, pre_s, act, slope, nrm, inv,
    e1, h1, msg, actn, slopen, nrmn, invn, hs, halo, tds, td_own, tarr,
    gh, ges, gedge, gpe, tab,
    AG, ssem, rsem, *rest,
):
    dp, me = lax.axis_index("dp"), lax.axis_index("mesh")
    core, x_lo, z = dp % 2, (dp // 2) % 2, dp // 4
    y, x_hi = me // 2, me % 2
    x = 2 * x_hi + x_lo

    partner = device(z, y, x, 1 - core)
    right = (device(z, y, (x + 1) % 4, core), device(z, (y + 1) % 4, x, core), device((z + 1) % 8, y, x, core))
    left = (device(z, y, (x + 3) % 4, core), device(z, (y + 3) % 4, x, core), device((z + 7) % 8, y, x, core))
    z_peers = [device((z + o) % 8, y, x, core) for o in range(1, 8)]
    plane = {
        (ox, oy): device(z, (y + oy) % 4, (x + ox) % 4, core)
        for ox in range(4) for oy in range(4) if ox or oy
    }
    mesh_peers = [(dp, (me + o) % 8) for o in range(1, 8)]
    greeted = z_peers + list(plane.values()) + [partner]
    barrier = pltpu.get_barrier_semaphore()
    for peer in greeted:
        pl.semaphore_signal(barrier, inc=1, device_id=peer, device_id_type=pl.DeviceIdType.MESH)

    loads = {}
    for l in range(L):
        for k, (src, dst) in enumerate(((wei_h, wei), (weo_h, weo), (wni_h, wni), (wno_h, wno))):
            loads[l, k] = pltpu.make_async_copy(src.at[l], dst.at[l], wsem.at[4 * l + k])
            loads[l, k].start()

    copies = []

    def push(src, dst, dev):
        n = len(copies)
        copy = pltpu.make_async_remote_copy(
            src_ref=src, dst_ref=dst, send_sem=ssem.at[n], recv_sem=rsem.at[n],
            device_id=dev, device_id_type=pl.DeviceIdType.MESH,
        )
        copy.start()
        copies.append(copy)
        return copy

    i0, i1 = iota((E, ND), 0), iota((E, ND), 1)
    s_dst = (i0 // K == i1).astype(F32)
    spread = nt(s_dst.astype(BF16), nb[...].astype(F32).astype(BF16))
    nbcol = jnp.sum(
        jnp.where(iota((E, K), 0) % K == iota((E, K), 1), spread, 0.0), axis=1, keepdims=True
    )
    s_src = (nbcol == iota((E, 128), 1).astype(F32)).astype(F32)
    S[:, 0:128] = s_src.astype(BF16)
    S[:, 128:192] = s_dst.astype(BF16)
    ST[0:128, :] = s_src.T.astype(BF16)
    ST[128:192, :] = (iota((ND, E), 1) // K == iota((ND, E), 0)).astype(F32).astype(BF16)
    countcol = jnp.sum(s_dst * cnt[...].astype(F32), axis=1, keepdims=True)
    live[...] = ((iota((E, 1), 0) % K).astype(F32) < countcol).astype(F32)
    oc[...] = jnp.sum(
        jnp.where(iota((ND, ND), 0) == iota((ND, ND), 1), oce[...].astype(F32), 0.0),
        axis=1, keepdims=True,
    )
    sendf = send[...].astype(F32)
    sendcol = jnp.sum(
        jnp.where(iota((2 * H, 2 * H), 0) == iota((2 * H, 2 * H), 1), sendf, 0.0),
        axis=1, keepdims=True,
    )
    SEND[...] = (sendcol == iota((2 * H, ND), 1).astype(F32)).astype(F32).astype(BF16)
    SENDT[...] = (sendf == iota((ND, 2 * H), 0).astype(F32)).astype(F32).astype(BF16)
    PQ[...] = jnp.zeros_like(PQ)

    before, after = (dp, (me + 7) % 8), (dp, (me + 1) % 8)

    def forward(l, h, e):
        hs[l] = nn(SEND[...], h[...]).astype(BF16)

        def local():
            loads[l, 0].wait()
            PQ[0:ND, :] = nn(h[...], wei[l, D : 2 * D]).astype(BF16)
            PQ[128:192, :] = nn(h[...], wei[l, 2 * D :]).astype(BF16)
            pre_s[...] = nn(e[...], wei[l, 0:D])
            loads[l, 1].wait()

        if l == 0:
            local()
            pl.semaphore_wait(barrier, len(greeted))
        first = push(hs.at[l, pl.ds(0, H)], halo.at[l, pl.ds(H, H)], before)
        second = push(hs.at[l, pl.ds(H, H)], halo.at[l, pl.ds(0, H)], after)
        if l:
            local()
        first.wait_recv()
        second.wait_recv()
        tab[l, 0:ND] = h[...]
        tab[l, ND : ND + 2 * H] = halo[l]
        tab[l, ND + 2 * H :] = jnp.zeros((32, D), BF16)
        PQ[ND : ND + 2 * H, :] = nn(halo[l], wei[l, D : 2 * D]).astype(BF16)
        for b in range(NBLK):
            r = slice(b * BLK, (b + 1) * BLK)
            pre = pre_s[r] + nn(S[r], PQ[...])
            a, sl = silu_parts(pre)
            act[l, r] = a
            slope[l, r] = sl
            n, v = norm_parts(nn(a, weo[l]))
            nrm[l, r] = n
            inv[l, r] = v
            lv = live[r]
            ne = (e[r].astype(F32) + lv * n).astype(BF16)
            if l + 1 < L:
                e1[r] = ne
            m = jnp.sum((lv * ne.astype(F32)).reshape(PER, K, D), axis=1)
            msg[l, b * PER : (b + 1) * PER] = m.astype(BF16)
        loads[l, 2].wait()
        loads[l, 3].wait()
        pre = nn(h[...], wni[l, 0:D]) + nn(msg[l], wni[l, D:])
        a, sl = silu_parts(pre)
        actn[l] = a
        slopen[l] = sl
        n, v = norm_parts(nn(a, wno[l]))
        nrmn[l] = n
        invn[l] = v
        if l + 1 < L:
            h1[...] = (h[...].astype(F32) + oc[...] * n).astype(BF16)

    forward(0, h0, e0)
    forward(1, h1, e1)

    bufs = iter(rest)
    G, C, RA, RB, T1, SB, T2, ZB = {}, {}, {}, {}, {}, {}, {}, {}
    for l in range(L):
        for c in range(3):
            names = (G, C, RA, RB, T1, SB, T2, ZB) if c < 2 else (G, C, RA, RB, T1, SB)
            for name in names:
                name[l, c] = next(bufs)

    def store_unit(l, kind, unit, val):
        per, base = ((3, 0), (1, 3), (2, 4), (1, 6))[kind]
        val = val.astype(BF16)
        for n in range(D // 16):
            at = unit * (D // 16) + n
            d, j = at // per, base + at % per
            dcore, dxl, dz = d % 2, (d // 2) % 2, d // 4
            c = [j in GROUPS[l][k] for k in range(3)].index(True)
            g = GROUPS[l][c].index(j)
            for dxh in range(2):
                for dy in range(4):
                    dx = 2 * dxh + dxl
                    place = ((dx, dy, dz), (dy, dx, dz), (dz, dx, dy))[c]
                    row = 16 * n + 8 * dxh
                    G[l, c][(dcore,) + place + (g,)] = val[row : row + 8, 128 * dy : 128 * dy + 128]

    gh[...] = nc[...].astype(F32)
    ges[...] = ec[...].astype(F32)

    def node_back(l, h):
        gout = norm_back(nrmn[l], invn[l], oc[...] * gh[...]).astype(BF16)
        gpre = (nt(gout, wno[l]) * slopen[l]).astype(BF16)
        gin = nt(gpre, wni[l])
        gh[...] = gh[...] + gin[:, 0:D]
        store_unit(l, 2, 0, tn(h[...], gpre))
        store_unit(l, 2, 1, tn(msg[l], gpre))
        store_unit(l, 3, 0, tn(actn[l], gout))
        return gin[:, D:]

    def edge_back(l, gm, e):
        for b in range(NBLK):
            r = slice(b * BLK, (b + 1) * BLK)
            lv = live[r]
            part = gm[b * PER : (b + 1) * PER]
            part = jnp.broadcast_to(part[:, None, :], (PER, K, D)).reshape(BLK, D)
            ge2 = ges[r] + lv * part
            g = norm_back(nrm[l, r], inv[l, r], lv * ge2).astype(BF16)
            gedge[r] = g
            gp = (nt(g, weo[l]) * slope[l, r]).astype(BF16)
            gpe[r] = gp
            new = ge2 + nt(gp, wei[l, 0:D])
            if l:
                ges[r] = new
            else:
                ge_out[r] = new.astype(BF16)

    def weights_a(l):
        td = tds.at[l]
        sums = nn(ST[...], gpe[...])
        td[...] = sums.astype(BF16)
        td_own[...] = sums[0:ND]
        first = push(td.at[pl.ds(ND, H)], tarr.at[l, pl.ds(H, H)], before)
        second = push(td.at[pl.ds(ND + H, H)], tarr.at[l, pl.ds(0, H)], after)
        store_unit(l, 1, 0, tn(act[l], gedge[...]))
        return first, second

    def weights_b(l, h, e):
        td = tds.at[l]
        store_unit(l, 0, 0, tn(e[...], gpe[...]))
        store_unit(l, 0, 1, tn(tab[l], td[0:128]))
        whole = 2 * D // (3 * 16) // 4
        sent = [[swap_part(l, c, pl.ds(0, whole))] for c in range(2)]
        store_unit(l, 0, 2, tn(h[...], td[128:192]))
        for c in range(2):
            sent[c].append(swap_part(l, c, pl.ds(whole, 8 - whole)))
        return sent

    def nodes_done(l, returned):
        td = tds.at[l]
        for m in returned:
            m.wait_recv()
        src = (td_own[...] + nn(SENDT[...], tarr[l])).astype(BF16)
        pre_s[0:ND] = nt(src, wei[l, D : 2 * D]) + nt(td[128:192], wei[l, 2 * D :])
        into = gh if l else gn_out

        @pl.loop(0, ND // 8)
        def _(i):
            r = pl.ds(pl.multiple_of(8 * i, 8), 8)
            into[r] = gh[r] + pre_s[r]

    pos = ((x, y), (y, x))

    def swap(l, c):
        return push(G[l, c].at[1 - core], C[l, c], partner)

    def swap_part(l, c, part):
        al = slice(None)
        return push(G[l, c].at[1 - core, al, al, part], C[l, c].at[al, al, part], partner)

    def settle(l, c, i, rows):
        for k in rows:
            G[l, c][core, i, k] = G[l, c][core, i, k] + C[l, c][i, k]

    def absorb(l, c, i, k, more):
        G[l, c][core, i, k] = G[l, c][core, i, k] + C[l, c][i, k] + more

    def total(l, c, i, k, one, two):
        own = G[l, c][core, i, k].astype(F32) + C[l, c][i, k].astype(F32)
        T1[l, c][k] = (own + (one.astype(F32) + two.astype(F32))).astype(BF16)

    def ring4(l, c, swapped):
        for m in swapped:
            m.wait_recv()
        ref, ra, rb = G[l, c], RA[l, c], RB[l, c]
        a = pos[c][0]
        r, o, q = (a + 1) % 4, (a + 2) % 4, (a + 3) % 4
        lo, hi = pl.ds(0, 2), pl.ds(2, 2)
        settle(l, c, o, (0, 1))
        m1r = push(ref.at[core, o, lo], ra.at[0], right[c])
        settle(l, c, o, (2, 3))
        m1l = push(ref.at[core, o, hi], ra.at[1], left[c])
        settle(l, c, r, (2, 3))
        m2r = push(ref.at[core, r, hi], rb.at[0, hi], right[c])
        settle(l, c, q, (0, 1))
        m2l = push(ref.at[core, q, lo], rb.at[1, lo], left[c])

        def relay():
            m1r.wait_recv()
            for i in range(2):
                absorb(l, c, r, i, ra[0, i])
            m3r = push(ref.at[core, r, lo], rb.at[0, lo], right[c])
            m1l.wait_recv()
            for i in range(2):
                absorb(l, c, q, 2 + i, ra[1, i])
            m3l = push(ref.at[core, q, hi], rb.at[1, hi], left[c])

            def close():
                for m in (m2r, m2l, m3r, m3l):
                    m.wait_recv()
                for i in range(4):
                    total(l, c, a, i, rb[0, i], rb[1, i])

            return close

        return relay

    def across(l, c):
        b = pos[c][1]
        t, s = T1[l, c], SB[l, c]
        peer = [plane[(0, o) if c == 0 else (o, 0)] for o in range(1, 4)]
        sent = [push(t.at[(b + o) % 4], s.at[o], peer[o - 1]) for o in range(1, 4)]

        def close():
            for m in sent:
                m.wait_recv()
            total = t[b].astype(F32)
            for o in range(1, 4):
                total = total + s[o].astype(F32)
            T2[l, c][...] = total.astype(BF16)

        return close

    def keep(l, c, total):
        for g, j in enumerate(GROUPS[l][c]):
            AG[l, me, j] = total[g].astype(BF16)

    def along(l, c):
        t, s = T2[l, c], ZB[l, c]
        sent = [push(t.at[(z + o) % 8], s.at[o], z_peers[o - 1]) for o in range(1, 8)]

        def close():
            for m in sent:
                m.wait_recv()
            total = t[z].astype(F32)
            for o in range(1, 8):
                total = total + s[o].astype(F32)
            keep(l, c, total)

        return close

    def ring8(l, swapped):
        swapped.wait_recv()
        ref, first, full = G[l, 2], RA[l, 2], RB[l, 2]
        lo, hi = pl.ds(0, 2), pl.ds(2, 2)
        far = (z + 4) % 8
        settle(l, 2, far, range(4))
        got = [
            push(ref.at[core, far, lo], first.at[0], right[2]),
            push(ref.at[core, far, hi], first.at[1], left[2]),
        ]

        def step(n):
            for way in range(2):
                at = (z + (4 - n if way == 0 else 4 + n)) % 8
                if n == 1:
                    settle(l, 2, at, (2 - 2 * way, 3 - 2 * way))
                got[way].wait_recv()
                for i in (2 * way, 2 * way + 1) if n == 1 else range(4):
                    absorb(l, 2, at, i, first[way, i % 2] if n == 1 else full[way, n - 2, i])
                got[way] = push(
                    ref.at[core, at], full.at[way, n - 1], (right, left)[way][2]
                )

        def close():
            for way in range(2):
                got[way].wait_recv()
            for i in range(4):
                total(l, 2, z, i, full[0, 2, i], full[1, 2, i])

        return step, close

    def spread_plane(l):
        t, s = T1[l, 2], SB[l, 2]
        sent = [
            push(t.at[(x + ox) % 4, (y + oy) % 4], s.at[ox, oy], dev) for (ox, oy), dev in plane.items()
        ]

        def close():
            for m in sent:
                m.wait_recv()
            total = t[x, y].astype(F32)
            for ox, oy in plane:
                total = total + s[ox, oy].astype(F32)
            keep(l, 2, total)

        return close

    def gather(l):
        return [push(AG.at[l, me], AG.at[l, me], peer) for peer in mesh_peers]

    def write(l, pushed):
        for m in pushed:
            m.wait_recv()
        wg_out[l] = AG[l]

    both = lambda fn, l: [fn(l, c) for c in range(2)]
    run = lambda fns: [fn() for fn in fns]

    drained = [0]

    def drain(upto):
        for copy in copies[drained[0] : upto]:
            copy.wait_send()
        drained[0] = upto

    gm = node_back(1, h1)
    swz1 = swap(1, 2)
    edge_back(1, gm, e1)
    z1, z1_close = ring8(1, swz1)
    back1 = weights_a(1)
    sw1 = weights_b(1, h1, e1)
    z1(1)
    nodes_done(1, back1)
    gm = node_back(0, h0)
    swz0 = swap(0, 2)
    z1(2)
    xy1 = [ring4(1, c, sw1[c]) for c in range(2)]
    edge_back(0, gm, e0)
    z1(3)
    xy1 = run(xy1)
    z0, z0_close = ring8(0, swz0)
    back0 = weights_a(0)
    run(xy1)
    xy1 = both(across, 1)
    z1_close()
    z1_end = spread_plane(1)
    sw0 = weights_b(0, h0, e0)
    early = len(copies)
    z0(1)
    run(xy1)
    xy1 = both(along, 1)
    xy0 = [ring4(0, c, sw0[c]) for c in range(2)]
    z0(2)
    nodes_done(0, back0)
    z1_end()
    xy0 = run(xy0)
    run(xy1)
    last1 = gather(1)
    z0(3)
    drain(early)
    run(xy0)
    xy0 = both(across, 0)
    z0_close()
    z0_end = spread_plane(0)
    write(1, last1)
    run(xy0)
    xy0 = both(along, 0)
    z0_end()
    drain(len(copies) - 14)
    run(xy0)
    last0 = gather(0)
    drain(len(copies) - 7)
    write(0, last0)
    drain(len(copies))


def body(
    node_feats, edge_feats, node_cot, edge_cot, w_edge_in, w_edge_out, w_node_in, w_node_out,
    neighbours, send_rows, edge_counts, ocean_mask,
):
    samples, nodes, features = node_feats.shape
    total_rows = samples * lax.axis_size("dp") * nodes * lax.axis_size("mesh")
    factor = 1.0 / total_rows**0.5
    vmem = pl.BlockSpec(memory_space=pltpu.VMEM)
    hbm = pl.BlockSpec(memory_space=pl.ANY)

    def buf(dtype, *shape):
        return pltpu.VMEM(shape, dtype)

    scratch = [
        buf(BF16, L, 3 * D, D), buf(BF16, L, D, D), buf(BF16, L, 2 * D, D), buf(BF16, L, D, D),
        pltpu.SemaphoreType.DMA((4 * L,)),
        buf(BF16, E, 192), buf(BF16, 192, E), buf(BF16, 2 * H, ND), buf(BF16, ND, 2 * H),
        buf(F32, E, 1), buf(F32, ND, 1), buf(BF16, 192, D), buf(F32, E, D),
        buf(BF16, L, E, D), buf(F32, L, E, D), buf(F32, L, E, D), buf(F32, L, E, 1),
        buf(BF16, E, D), buf(BF16, ND, D), buf(BF16, L, ND, D),
        buf(BF16, L, ND, D), buf(F32, L, ND, D), buf(F32, L, ND, D), buf(F32, L, ND, 1),
        buf(BF16, L, 2 * H, D), buf(BF16, L, 2 * H, D),
        buf(BF16, L, 192, D), buf(F32, ND, D), buf(BF16, L, 2 * H, D),
        buf(F32, ND, D), buf(F32, E, D), buf(BF16, E, D), buf(BF16, E, D), buf(BF16, L, 128, D),
        buf(BF16, L, 8, 7, 8, 128),
        pltpu.SemaphoreType.DMA((NSEM,)), pltpu.SemaphoreType.DMA((NSEM,)),
    ]
    for l in range(L):
        for c in range(3):
            tile = (len(GROUPS[l][c]), 8, 128)
            if c < 2:
                shapes = (
                    (2, 4, 4, 8), (4, 4, 8), (2, 2, 8), (2, 4, 8), (4, 8), (4, 8), (8,), (8,),
                )
            else:
                shapes = ((2, 8, 4, 4), (8, 4, 4), (2, 2, 4), (2, 3, 4, 4), (4, 4), (4, 4))
            scratch += [buf(BF16, *(shape + tile)) for shape in shapes]

    done = pl.pallas_call(
        kernel,
        out_shape=(
            jax.ShapeDtypeStruct((ND, D), F32),
            jax.ShapeDtypeStruct((E, D), BF16),
            jax.ShapeDtypeStruct((L, 8, 7, 8, 128), BF16),
        ),
        in_specs=[vmem] * 4 + [hbm] * 4 + [vmem] * 4,
        out_specs=(vmem,) * 3,
        scratch_shapes=scratch,
        compiler_params=pltpu.CompilerParams(
            collective_id=0, has_side_effects=True, vmem_limit_bytes=60 << 20
        ),
    )(
        node_feats.reshape(ND, D), edge_feats.reshape(E, D),
        node_cot.reshape(ND, D), edge_cot.reshape(E, D),
        w_edge_in, w_edge_out, w_node_in, w_node_out,
        neighbours.T, send_rows, edge_counts.reshape(1, ND), ocean_mask.reshape(1, ND),
    )

    def finish(gn, ge, wg, gn_out, ge_out, oei, oeo, oni, ono):
        gn_out[...] = gn[...]
        ge_out[...] = ge[...]
        for l in range(L):
            for j in range(7):
                ref, row = ((oei, j), (oei, j), (oei, j), (oeo, 0), (oni, 0), (oni, 1), (ono, 0))[j]
                for m in range(8):
                    r, q = 16 * row + 8 * (m % 2), 128 * (m // 2)
                    ref[l, r : r + 8, q : q + 128] = wg[l, m, j].astype(F32) * factor

    outs = pl.pallas_call(
        finish,
        out_shape=(
            jax.ShapeDtypeStruct((ND, D), F32),
            jax.ShapeDtypeStruct((E, D), BF16),
            jax.ShapeDtypeStruct((L, 48, D), F32),
            jax.ShapeDtypeStruct((L, 16, D), F32),
            jax.ShapeDtypeStruct((L, 32, D), F32),
            jax.ShapeDtypeStruct((L, 16, D), F32),
        ),
        in_specs=[vmem] * 3,
        out_specs=(vmem,) * 6,
    )(*done)
    return (outs[0].reshape(samples, nodes, D), outs[1].reshape(samples, nodes, K, D)) + tuple(outs[2:])


def solution(mesh):
    rows, edges = P("dp", "mesh", None), P("dp", "mesh", None, None)
    weight = P(None, "dp", None)
    return jax.shard_map(
        body,
        mesh=mesh,
        in_specs=(
            rows, edges, rows, edges, P(), P(), P(), P(),
            P("mesh", None), P("mesh", None), P("mesh"), P("mesh"),
        ),
        out_specs=(rows, edges, weight, weight, weight, weight),
        check_vma=False,
    )
```

```python
import jax
import jax.numpy as jnp
from jax import lax
from jax.experimental import pallas as pl
from jax.experimental.pallas import tpu as pltpu
from jax.sharding import PartitionSpec as P

F32, BF16 = jnp.float32, jnp.bfloat16
D, K, L, ND, H = 512, 8, 2, 64, 16
E = ND * K
BLK = 256
NBLK = E // BLK
PER = BLK // K
EPS = 1e-05
NSEM = 144
GROUPS = (((0, 3), (1, 2), (4, 5, 6)),) * L


def nn(a, b):
    return lax.dot_general(a, b, (((1,), (0,)), ((), ())), preferred_element_type=F32)


def nt(a, b):
    return lax.dot_general(a, b, (((1,), (1,)), ((), ())), preferred_element_type=F32)


def tn(a, b):
    return lax.dot_general(a, b, (((0,), (0,)), ((), ())), preferred_element_type=F32)


def iota(shape, axis):
    return lax.broadcasted_iota(jnp.int32, shape, axis)


def row_mean(v):
    return jnp.sum(v, axis=-1, keepdims=True) * (1.0 / D)


def silu_parts(pre):
    sig = 0.5 * jnp.tanh(0.5 * pre) + 0.5
    return (pre * sig).astype(BF16), sig * (1.0 + pre * (1.0 - sig))


def norm_parts(v):
    shifted = v - row_mean(v)
    inverse = lax.rsqrt(row_mean(shifted * shifted) + EPS)
    return shifted * inverse, inverse


def norm_back(normed, inverse, up):
    return inverse * (up - row_mean(up) - normed * row_mean(up * normed))


def device(z, y, x, core):
    return (z * 2 + x % 2) * 2 + core, y * 2 + x // 2


def kernel(
    h0, e0, nc, ec, wei_h, weo_h, wni_h, wno_h, nb, send, cnt, oce,
    gn_out, ge_out, wg_out,
    wei, weo, wni, wno, wsem,
    S, ST, SEND, SENDT, live, oc, PQ, pre_s, act, slope, nrm, inv,
    e1, h1, msg, actn, slopen, nrmn, invn, hs, halo, tds, td_own, tarr,
    gh, ges, gedge, gpe, tab,
    AG, ssem, rsem, *rest,
):
    dp, me = lax.axis_index("dp"), lax.axis_index("mesh")
    core, x_lo, z = dp % 2, (dp // 2) % 2, dp // 4
    y, x_hi = me // 2, me % 2
    x = 2 * x_hi + x_lo

    partner = device(z, y, x, 1 - core)
    right = (device(z, y, (x + 1) % 4, core), device(z, (y + 1) % 4, x, core), device((z + 1) % 8, y, x, core))
    left = (device(z, y, (x + 3) % 4, core), device(z, (y + 3) % 4, x, core), device((z + 7) % 8, y, x, core))
    z_peers = [device((z + o) % 8, y, x, core) for o in range(1, 8)]
    plane = {
        (ox, oy): device(z, (y + oy) % 4, (x + ox) % 4, core)
        for ox in range(4) for oy in range(4) if ox or oy
    }
    mesh_peers = [(dp, (me + o) % 8) for o in range(1, 8)]
    greeted = z_peers + list(plane.values()) + [partner]
    barrier = pltpu.get_barrier_semaphore()
    for peer in greeted:
        pl.semaphore_signal(barrier, inc=1, device_id=peer, device_id_type=pl.DeviceIdType.MESH)

    loads = {}
    for l in range(L):
        for k, (src, dst) in enumerate(((wei_h, wei), (weo_h, weo), (wni_h, wni), (wno_h, wno))):
            loads[l, k] = pltpu.make_async_copy(src.at[l], dst.at[l], wsem.at[4 * l + k])
            loads[l, k].start()

    copies = []

    def push(src, dst, dev):
        n = len(copies)
        copy = pltpu.make_async_remote_copy(
            src_ref=src, dst_ref=dst, send_sem=ssem.at[n], recv_sem=rsem.at[n],
            device_id=dev, device_id_type=pl.DeviceIdType.MESH,
        )
        copy.start()
        copies.append(copy)
        return copy

    i0, i1 = iota((E, ND), 0), iota((E, ND), 1)
    s_dst = (i0 // K == i1).astype(F32)
    spread = nt(s_dst.astype(BF16), nb[...].astype(F32).astype(BF16))
    nbcol = jnp.sum(
        jnp.where(iota((E, K), 0) % K == iota((E, K), 1), spread, 0.0), axis=1, keepdims=True
    )
    s_src = (nbcol == iota((E, 128), 1).astype(F32)).astype(F32)
    S[:, 0:128] = s_src.astype(BF16)
    S[:, 128:192] = s_dst.astype(BF16)
    ST[0:128, :] = s_src.T.astype(BF16)
    ST[128:192, :] = (iota((ND, E), 1) // K == iota((ND, E), 0)).astype(F32).astype(BF16)
    countcol = jnp.sum(s_dst * cnt[...].astype(F32), axis=1, keepdims=True)
    live[...] = ((iota((E, 1), 0) % K).astype(F32) < countcol).astype(F32)
    oc[...] = jnp.sum(
        jnp.where(iota((ND, ND), 0) == iota((ND, ND), 1), oce[...].astype(F32), 0.0),
        axis=1, keepdims=True,
    )
    sendf = send[...].astype(F32)
    sendcol = jnp.sum(
        jnp.where(iota((2 * H, 2 * H), 0) == iota((2 * H, 2 * H), 1), sendf, 0.0),
        axis=1, keepdims=True,
    )
    SEND[...] = (sendcol == iota((2 * H, ND), 1).astype(F32)).astype(F32).astype(BF16)
    SENDT[...] = (sendf == iota((ND, 2 * H), 0).astype(F32)).astype(F32).astype(BF16)
    PQ[...] = jnp.zeros_like(PQ)

    before, after = (dp, (me + 7) % 8), (dp, (me + 1) % 8)

    def forward(l, h, e):
        hs[l] = nn(SEND[...], h[...]).astype(BF16)

        def local():
            loads[l, 0].wait()
            PQ[0:ND, :] = nn(h[...], wei[l, D : 2 * D]).astype(BF16)
            PQ[128:192, :] = nn(h[...], wei[l, 2 * D :]).astype(BF16)
            pre_s[...] = nn(e[...], wei[l, 0:D])
            loads[l, 1].wait()

        if l == 0:
            local()
            pl.semaphore_wait(barrier, len(greeted))
        first = push(hs.at[l, pl.ds(0, H)], halo.at[l, pl.ds(H, H)], before)
        second = push(hs.at[l, pl.ds(H, H)], halo.at[l, pl.ds(0, H)], after)
        if l:
            local()
        else:
            gh[...] = nc[...].astype(F32)
            ges[...] = ec[...].astype(F32)
        loads[l, 2].wait()
        td_own[...] = nn(h[...], wni[l, 0:D])
        first.wait_recv()
        second.wait_recv()
        tab[l, 0:ND] = h[...]
        tab[l, ND : ND + 2 * H] = halo[l]
        tab[l, ND + 2 * H :] = jnp.zeros((32, D), BF16)
        PQ[ND : ND + 2 * H, :] = nn(halo[l], wei[l, D : 2 * D]).astype(BF16)
        for b in range(NBLK):
            r = slice(b * BLK, (b + 1) * BLK)
            pre = pre_s[r] + nn(S[r], PQ[...])
            a, sl = silu_parts(pre)
            act[l, r] = a
            slope[l, r] = sl
            n, v = norm_parts(nn(a, weo[l]))
            nrm[l, r] = n
            inv[l, r] = v
            lv = live[r]
            ne = (e[r].astype(F32) + lv * n).astype(BF16)
            if l + 1 < L:
                e1[r] = ne
            m = jnp.sum((lv * ne.astype(F32)).reshape(PER, K, D), axis=1)
            msg[l, b * PER : (b + 1) * PER] = m.astype(BF16)
        loads[l, 3].wait()
        pre = td_own[...] + nn(msg[l], wni[l, D:])
        a, sl = silu_parts(pre)
        actn[l] = a
        slopen[l] = sl
        n, v = norm_parts(nn(a, wno[l]))
        nrmn[l] = n
        invn[l] = v
        if l + 1 < L:
            h1[...] = (h[...].astype(F32) + oc[...] * n).astype(BF16)

    forward(0, h0, e0)
    forward(1, h1, e1)

    bufs = iter(rest)
    G, C, RA, RB, T1, SB, T2, ZB = {}, {}, {}, {}, {}, {}, {}, {}
    for l in range(L):
        for c in range(3):
            names = (G, C, RA, RB, T1, SB, T2, ZB) if c < 2 else (G, C, RA, RB, T1, SB)
            for name in names:
                name[l, c] = next(bufs)

    def store_unit(l, kind, unit, val):
        per, base = ((3, 0), (1, 3), (2, 4), (1, 6))[kind]
        val = val.astype(BF16)
        for n in range(D // 16):
            at = unit * (D // 16) + n
            d, j = at // per, base + at % per
            dcore, dxl, dz = d % 2, (d // 2) % 2, d // 4
            c = [j in GROUPS[l][k] for k in range(3)].index(True)
            g = GROUPS[l][c].index(j)
            for dxh in range(2):
                for dy in range(4):
                    dx = 2 * dxh + dxl
                    place = ((dx, dy, dz), (dy, dx, dz), (dz, dx, dy))[c]
                    row = 16 * n + 8 * dxh
                    G[l, c][(dcore,) + place + (g,)] = val[row : row + 8, 128 * dy : 128 * dy + 128]


    def node_back(l, h):
        gout = norm_back(nrmn[l], invn[l], oc[...] * gh[...]).astype(BF16)
        gpre = (nt(gout, wno[l]) * slopen[l]).astype(BF16)
        gin = nt(gpre, wni[l])
        gh[...] = gh[...] + gin[:, 0:D]
        store_unit(l, 2, 0, tn(h[...], gpre))
        store_unit(l, 2, 1, tn(msg[l], gpre))
        store_unit(l, 3, 0, tn(actn[l], gout))
        return gin[:, D:]

    def edge_back(l, gm, e):
        for b in range(NBLK):
            r = slice(b * BLK, (b + 1) * BLK)
            lv = live[r]
            part = gm[b * PER : (b + 1) * PER]
            part = jnp.broadcast_to(part[:, None, :], (PER, K, D)).reshape(BLK, D)
            ge2 = ges[r] + lv * part
            g = norm_back(nrm[l, r], inv[l, r], lv * ge2).astype(BF16)
            gedge[r] = g
            gp = (nt(g, weo[l]) * slope[l, r]).astype(BF16)
            gpe[r] = gp
            new = ge2 + nt(gp, wei[l, 0:D])
            if l:
                ges[r] = new
            else:
                ge_out[r] = new.astype(BF16)

    def weights_a(l):
        td = tds.at[l]
        sums = nn(ST[...], gpe[...])
        td[...] = sums.astype(BF16)
        td_own[...] = sums[0:ND]
        first = push(td.at[pl.ds(ND, H)], tarr.at[l, pl.ds(H, H)], before)
        second = push(td.at[pl.ds(ND + H, H)], tarr.at[l, pl.ds(0, H)], after)
        store_unit(l, 1, 0, tn(act[l], gedge[...]))
        return first, second

    def weights_b(l, h, e):
        td = tds.at[l]
        store_unit(l, 0, 0, tn(e[...], gpe[...]))
        store_unit(l, 0, 1, tn(tab[l], td[0:128]))
        whole = 2 * D // (3 * 16) // 4
        sent = [[swap_part(l, c, pl.ds(0, whole))] for c in range(2)]
        store_unit(l, 0, 2, tn(h[...], td[128:192]))
        for c in range(2):
            sent[c].append(swap_part(l, c, pl.ds(whole, 8 - whole)))
        return sent

    def nodes_done(l, returned):
        td = tds.at[l]
        for m in returned:
            m.wait_recv()
        src = (td_own[...] + nn(SENDT[...], tarr[l])).astype(BF16)
        pre_s[0:ND] = nt(src, wei[l, D : 2 * D]) + nt(td[128:192], wei[l, 2 * D :])
        into = gh if l else gn_out

        @pl.loop(0, ND // 8)
        def _(i):
            r = pl.ds(pl.multiple_of(8 * i, 8), 8)
            into[r] = gh[r] + pre_s[r]

    pos = ((x, y), (y, x))

    def swap(l, c):
        return push(G[l, c].at[1 - core], C[l, c], partner)

    def swap_part(l, c, part):
        al = slice(None)
        return push(G[l, c].at[1 - core, al, al, part], C[l, c].at[al, al, part], partner)

    def settle(l, c, i, rows):
        for k in rows:
            G[l, c][core, i, k] = G[l, c][core, i, k] + C[l, c][i, k]

    def absorb(l, c, i, k, more):
        G[l, c][core, i, k] = G[l, c][core, i, k] + C[l, c][i, k] + more

    def total(l, c, i, k, one, two):
        own = G[l, c][core, i, k].astype(F32) + C[l, c][i, k].astype(F32)
        T1[l, c][k] = (own + (one.astype(F32) + two.astype(F32))).astype(BF16)

    def ring4(l, c, swapped):
        for m in swapped:
            m.wait_recv()
        ref, ra, rb = G[l, c], RA[l, c], RB[l, c]
        a = pos[c][0]
        r, o, q = (a + 1) % 4, (a + 2) % 4, (a + 3) % 4
        lo, hi = pl.ds(0, 2), pl.ds(2, 2)
        settle(l, c, o, (0, 1))
        m1r = push(ref.at[core, o, lo], ra.at[0], right[c])
        settle(l, c, o, (2, 3))
        m1l = push(ref.at[core, o, hi], ra.at[1], left[c])
        settle(l, c, r, (2, 3))
        m2r = push(ref.at[core, r, hi], rb.at[0, hi], right[c])
        settle(l, c, q, (0, 1))
        m2l = push(ref.at[core, q, lo], rb.at[1, lo], left[c])

        def relay():
            m1r.wait_recv()
            for i in range(2):
                absorb(l, c, r, i, ra[0, i])
            m3r = push(ref.at[core, r, lo], rb.at[0, lo], right[c])
            m1l.wait_recv()
            for i in range(2):
                absorb(l, c, q, 2 + i, ra[1, i])
            m3l = push(ref.at[core, q, hi], rb.at[1, hi], left[c])

            def close():
                for m in (m2r, m2l, m3r, m3l):
                    m.wait_recv()
                for i in range(4):
                    total(l, c, a, i, rb[0, i], rb[1, i])

            return close

        return relay

    def across(l, c):
        b = pos[c][1]
        t, s = T1[l, c], SB[l, c]
        peer = [plane[(0, o) if c == 0 else (o, 0)] for o in range(1, 4)]
        sent = [push(t.at[(b + o) % 4], s.at[o], peer[o - 1]) for o in range(1, 4)]

        def close():
            for m in sent:
                m.wait_recv()
            total = t[b].astype(F32)
            for o in range(1, 4):
                total = total + s[o].astype(F32)
            T2[l, c][...] = total.astype(BF16)

        return close

    def keep(l, c, total):
        for g, j in enumerate(GROUPS[l][c]):
            AG[l, me, j] = total[g].astype(BF16)

    def along(l, c):
        t, s = T2[l, c], ZB[l, c]
        sent = [push(t.at[(z + o) % 8], s.at[o], z_peers[o - 1]) for o in range(1, 8)]

        def close():
            for m in sent:
                m.wait_recv()
            total = t[z].astype(F32)
            for o in range(1, 8):
                total = total + s[o].astype(F32)
            keep(l, c, total)

        return close

    def ring8(l, swapped):
        swapped.wait_recv()
        ref, first, full = G[l, 2], RA[l, 2], RB[l, 2]
        lo, hi = pl.ds(0, 2), pl.ds(2, 2)
        far = (z + 4) % 8
        settle(l, 2, far, range(4))
        got = [
            push(ref.at[core, far, lo], first.at[0], right[2]),
            push(ref.at[core, far, hi], first.at[1], left[2]),
        ]

        def step(n):
            for way in range(2):
                at = (z + (4 - n if way == 0 else 4 + n)) % 8
                if n == 1:
                    settle(l, 2, at, (2 - 2 * way, 3 - 2 * way))
                got[way].wait_recv()
                for i in (2 * way, 2 * way + 1) if n == 1 else range(4):
                    absorb(l, 2, at, i, first[way, i % 2] if n == 1 else full[way, n - 2, i])
                got[way] = push(
                    ref.at[core, at], full.at[way, n - 1], (right, left)[way][2]
                )

        def close():
            for way in range(2):
                got[way].wait_recv()
            for i in range(4):
                total(l, 2, z, i, full[0, 2, i], full[1, 2, i])

        return step, close

    def spread_plane(l):
        t, s = T1[l, 2], SB[l, 2]
        sent = [
            push(t.at[(x + ox) % 4, (y + oy) % 4], s.at[ox, oy], dev) for (ox, oy), dev in plane.items()
        ]

        def close():
            for m in sent:
                m.wait_recv()
            total = t[x, y].astype(F32)
            for ox, oy in plane:
                total = total + s[ox, oy].astype(F32)
            keep(l, 2, total)

        return close

    def gather(l):
        return [push(AG.at[l, me], AG.at[l, me], peer) for peer in mesh_peers]

    def write(l, pushed):
        for m in pushed:
            m.wait_recv()
        wg_out[l] = AG[l]

    both = lambda fn, l: [fn(l, c) for c in range(2)]
    run = lambda fns: [fn() for fn in fns]

    drained = [0]

    def drain(upto):
        for copy in copies[drained[0] : upto]:
            copy.wait_send()
        drained[0] = upto

    gm = node_back(1, h1)
    swz1 = swap(1, 2)
    edge_back(1, gm, e1)
    z1, z1_close = ring8(1, swz1)
    back1 = weights_a(1)
    sw1 = weights_b(1, h1, e1)
    z1(1)
    nodes_done(1, back1)
    gm = node_back(0, h0)
    swz0 = swap(0, 2)
    z1(2)
    xy1 = [ring4(1, c, sw1[c]) for c in range(2)]
    edge_back(0, gm, e0)
    z1(3)
    xy1 = run(xy1)
    z0, z0_close = ring8(0, swz0)
    back0 = weights_a(0)
    run(xy1)
    xy1 = both(across, 1)
    z1_close()
    z1_end = spread_plane(1)
    sw0 = weights_b(0, h0, e0)
    early = len(copies)
    z0(1)
    run(xy1)
    xy1 = both(along, 1)
    xy0 = [ring4(0, c, sw0[c]) for c in range(2)]
    z0(2)
    z1_end()
    xy0 = run(xy0)
    run(xy1)
    last1 = gather(1)
    z0(3)
    drain(early)
    run(xy0)
    xy0 = both(across, 0)
    z0_close()
    z0_end = spread_plane(0)
    nodes_done(0, back0)
    write(1, last1)
    run(xy0)
    xy0 = both(along, 0)
    z0_end()
    drain(len(copies) - 14)
    run(xy0)
    last0 = gather(0)
    drain(len(copies) - 7)
    write(0, last0)
    drain(len(copies))


def body(
    node_feats, edge_feats, node_cot, edge_cot, w_edge_in, w_edge_out, w_node_in, w_node_out,
    neighbours, send_rows, edge_counts, ocean_mask,
):
    samples, nodes, features = node_feats.shape
    total_rows = samples * lax.axis_size("dp") * nodes * lax.axis_size("mesh")
    factor = 1.0 / total_rows**0.5
    vmem = pl.BlockSpec(memory_space=pltpu.VMEM)
    hbm = pl.BlockSpec(memory_space=pl.ANY)

    def buf(dtype, *shape):
        return pltpu.VMEM(shape, dtype)

    scratch = [
        buf(BF16, L, 3 * D, D), buf(BF16, L, D, D), buf(BF16, L, 2 * D, D), buf(BF16, L, D, D),
        pltpu.SemaphoreType.DMA((4 * L,)),
        buf(BF16, E, 192), buf(BF16, 192, E), buf(BF16, 2 * H, ND), buf(BF16, ND, 2 * H),
        buf(F32, E, 1), buf(F32, ND, 1), buf(BF16, 192, D), buf(F32, E, D),
        buf(BF16, L, E, D), buf(F32, L, E, D), buf(F32, L, E, D), buf(F32, L, E, 1),
        buf(BF16, E, D), buf(BF16, ND, D), buf(BF16, L, ND, D),
        buf(BF16, L, ND, D), buf(F32, L, ND, D), buf(F32, L, ND, D), buf(F32, L, ND, 1),
        buf(BF16, L, 2 * H, D), buf(BF16, L, 2 * H, D),
        buf(BF16, L, 192, D), buf(F32, ND, D), buf(BF16, L, 2 * H, D),
        buf(F32, ND, D), buf(F32, E, D), buf(BF16, E, D), buf(BF16, E, D), buf(BF16, L, 128, D),
        buf(BF16, L, 8, 7, 8, 128),
        pltpu.SemaphoreType.DMA((NSEM,)), pltpu.SemaphoreType.DMA((NSEM,)),
    ]
    for l in range(L):
        for c in range(3):
            tile = (len(GROUPS[l][c]), 8, 128)
            if c < 2:
                shapes = (
                    (2, 4, 4, 8), (4, 4, 8), (2, 2, 8), (2, 4, 8), (4, 8), (4, 8), (8,), (8,),
                )
            else:
                shapes = ((2, 8, 4, 4), (8, 4, 4), (2, 2, 4), (2, 3, 4, 4), (4, 4), (4, 4))
            scratch += [buf(BF16, *(shape + tile)) for shape in shapes]

    done = pl.pallas_call(
        kernel,
        out_shape=(
            jax.ShapeDtypeStruct((ND, D), F32),
            jax.ShapeDtypeStruct((E, D), BF16),
            jax.ShapeDtypeStruct((L, 8, 7, 8, 128), BF16),
        ),
        in_specs=[vmem] * 4 + [hbm] * 4 + [vmem] * 4,
        out_specs=(vmem,) * 3,
        scratch_shapes=scratch,
        compiler_params=pltpu.CompilerParams(
            collective_id=0, has_side_effects=True, vmem_limit_bytes=60 << 20
        ),
    )(
        node_feats.reshape(ND, D), edge_feats.reshape(E, D),
        node_cot.reshape(ND, D), edge_cot.reshape(E, D),
        w_edge_in, w_edge_out, w_node_in, w_node_out,
        neighbours.T, send_rows, edge_counts.reshape(1, ND), ocean_mask.reshape(1, ND),
    )

    def finish(gn, ge, wg, gn_out, ge_out, oei, oeo, oni, ono):
        gn_out[...] = gn[...]
        ge_out[...] = ge[...]
        for l in range(L):
            for j in range(7):
                ref, row = ((oei, j), (oei, j), (oei, j), (oeo, 0), (oni, 0), (oni, 1), (ono, 0))[j]
                for m in range(8):
                    r, q = 16 * row + 8 * (m % 2), 128 * (m // 2)
                    ref[l, r : r + 8, q : q + 128] = wg[l, m, j].astype(F32) * factor

    outs = pl.pallas_call(
        finish,
        out_shape=(
            jax.ShapeDtypeStruct((ND, D), F32),
            jax.ShapeDtypeStruct((E, D), BF16),
            jax.ShapeDtypeStruct((L, 48, D), F32),
            jax.ShapeDtypeStruct((L, 16, D), F32),
            jax.ShapeDtypeStruct((L, 32, D), F32),
            jax.ShapeDtypeStruct((L, 16, D), F32),
        ),
        in_specs=[vmem] * 3,
        out_specs=(vmem,) * 6,
    )(*done)
    return (outs[0].reshape(samples, nodes, D), outs[1].reshape(samples, nodes, K, D)) + tuple(outs[2:])


def solution(mesh):
    rows, edges = P("dp", "mesh", None), P("dp", "mesh", None, None)
    weight = P(None, "dp", None)
    return jax.shard_map(
        body,
        mesh=mesh,
        in_specs=(
            rows, edges, rows, edges, P(), P(), P(), P(),
            P("mesh", None), P("mesh", None), P("mesh"), P("mesh"),
        ),
        out_specs=(rows, edges, weight, weight, weight, weight),
        check_vma=False,
    )
```

```python
import jax
import jax.numpy as jnp
from jax import lax
from jax.experimental import pallas as pl
from jax.experimental.pallas import tpu as pltpu
from jax.sharding import PartitionSpec as P

F32, BF16 = jnp.float32, jnp.bfloat16
D, K, L, ND, H = 512, 8, 2, 64, 16
E = ND * K
BLK = 512
NBLK = E // BLK
PER = BLK // K
EPS = 1e-05
NSEM = 144
GROUPS = (((0, 3), (1, 2), (4, 5, 6)),) * L


def nn(a, b):
    return lax.dot_general(a, b, (((1,), (0,)), ((), ())), preferred_element_type=F32)


def nt(a, b):
    return lax.dot_general(a, b, (((1,), (1,)), ((), ())), preferred_element_type=F32)


def tn(a, b):
    return lax.dot_general(a, b, (((0,), (0,)), ((), ())), preferred_element_type=F32)


def iota(shape, axis):
    return lax.broadcasted_iota(jnp.int32, shape, axis)


def row_mean(v):
    return jnp.sum(v, axis=-1, keepdims=True) * (1.0 / D)


def silu_parts(pre):
    sig = 0.5 * jnp.tanh(0.5 * pre) + 0.5
    return (pre * sig).astype(BF16), sig * (1.0 + pre * (1.0 - sig))


def norm_parts(v):
    shifted = v - row_mean(v)
    inverse = lax.rsqrt(row_mean(shifted * shifted) + EPS)
    return shifted * inverse, inverse


def norm_back(normed, inverse, up):
    return inverse * (up - row_mean(up) - normed * row_mean(up * normed))


def device(z, y, x, core):
    return (z * 2 + x % 2) * 2 + core, y * 2 + x // 2


def kernel(
    h0, e0, nc, ec, wei_h, weo_h, wni_h, wno_h, nb, send, cnt, oce,
    gn_out, ge_out, wg_out,
    wei, weo, wni, wno, wsem,
    S, ST, SEND, SENDT, live, oc, PQ, pre_s, act, slope, nrm, inv,
    e1, h1, msg, actn, slopen, nrmn, invn, hs, halo, tds, td_own, tarr,
    gh, ges, gedge, gpe, tab,
    AG, ssem, rsem, *rest,
):
    dp, me = lax.axis_index("dp"), lax.axis_index("mesh")
    core, x_lo, z = dp % 2, (dp // 2) % 2, dp // 4
    y, x_hi = me // 2, me % 2
    x = 2 * x_hi + x_lo

    partner = device(z, y, x, 1 - core)
    right = (device(z, y, (x + 1) % 4, core), device(z, (y + 1) % 4, x, core), device((z + 1) % 8, y, x, core))
    left = (device(z, y, (x + 3) % 4, core), device(z, (y + 3) % 4, x, core), device((z + 7) % 8, y, x, core))
    z_peers = [device((z + o) % 8, y, x, core) for o in range(1, 8)]
    plane = {
        (ox, oy): device(z, (y + oy) % 4, (x + ox) % 4, core)
        for ox in range(4) for oy in range(4) if ox or oy
    }
    mesh_peers = [(dp, (me + o) % 8) for o in range(1, 8)]
    greeted = z_peers + list(plane.values()) + [partner]
    barrier = pltpu.get_barrier_semaphore()
    for peer in greeted:
        pl.semaphore_signal(barrier, inc=1, device_id=peer, device_id_type=pl.DeviceIdType.MESH)

    loads = {}
    for l in range(L):
        for k, (src, dst) in enumerate(((wei_h, wei), (weo_h, weo), (wni_h, wni), (wno_h, wno))):
            loads[l, k] = pltpu.make_async_copy(src.at[l], dst.at[l], wsem.at[4 * l + k])
            loads[l, k].start()

    copies = []

    def push(src, dst, dev):
        n = len(copies)
        copy = pltpu.make_async_remote_copy(
            src_ref=src, dst_ref=dst, send_sem=ssem.at[n], recv_sem=rsem.at[n],
            device_id=dev, device_id_type=pl.DeviceIdType.MESH,
        )
        copy.start()
        copies.append(copy)
        return copy

    i0, i1 = iota((E, ND), 0), iota((E, ND), 1)
    s_dst = (i0 // K == i1).astype(F32)
    spread = nt(s_dst.astype(BF16), nb[...].astype(F32).astype(BF16))
    nbcol = jnp.sum(
        jnp.where(iota((E, K), 0) % K == iota((E, K), 1), spread, 0.0), axis=1, keepdims=True
    )
    s_src = (nbcol == iota((E, 128), 1).astype(F32)).astype(F32)
    S[:, 0:128] = s_src.astype(BF16)
    S[:, 128:192] = s_dst.astype(BF16)
    ST[0:128, :] = s_src.T.astype(BF16)
    ST[128:192, :] = (iota((ND, E), 1) // K == iota((ND, E), 0)).astype(F32).astype(BF16)
    countcol = jnp.sum(s_dst * cnt[...].astype(F32), axis=1, keepdims=True)
    live[...] = ((iota((E, 1), 0) % K).astype(F32) < countcol).astype(F32)
    oc[...] = jnp.sum(
        jnp.where(iota((ND, ND), 0) == iota((ND, ND), 1), oce[...].astype(F32), 0.0),
        axis=1, keepdims=True,
    )
    sendf = send[...].astype(F32)
    sendcol = jnp.sum(
        jnp.where(iota((2 * H, 2 * H), 0) == iota((2 * H, 2 * H), 1), sendf, 0.0),
        axis=1, keepdims=True,
    )
    SEND[...] = (sendcol == iota((2 * H, ND), 1).astype(F32)).astype(F32).astype(BF16)
    SENDT[...] = (sendf == iota((ND, 2 * H), 0).astype(F32)).astype(F32).astype(BF16)
    PQ[...] = jnp.zeros_like(PQ)

    before, after = (dp, (me + 7) % 8), (dp, (me + 1) % 8)

    def forward(l, h, e):
        hs[l] = nn(SEND[...], h[...]).astype(BF16)

        def local():
            loads[l, 0].wait()
            PQ[0:ND, :] = nn(h[...], wei[l, D : 2 * D]).astype(BF16)
            PQ[128:192, :] = nn(h[...], wei[l, 2 * D :]).astype(BF16)
            pre_s[...] = nn(e[...], wei[l, 0:D])
            loads[l, 1].wait()

        if l == 0:
            local()
            pl.semaphore_wait(barrier, len(greeted))
        first = push(hs.at[l, pl.ds(0, H)], halo.at[l, pl.ds(H, H)], before)
        second = push(hs.at[l, pl.ds(H, H)], halo.at[l, pl.ds(0, H)], after)
        if l:
            local()
        else:
            gh[...] = nc[...].astype(F32)
            ges[...] = ec[...].astype(F32)
        loads[l, 2].wait()
        td_own[...] = nn(h[...], wni[l, 0:D])
        first.wait_recv()
        second.wait_recv()
        tab[l, 0:ND] = h[...]
        tab[l, ND : ND + 2 * H] = halo[l]
        tab[l, ND + 2 * H :] = jnp.zeros((32, D), BF16)
        PQ[ND : ND + 2 * H, :] = nn(halo[l], wei[l, D : 2 * D]).astype(BF16)
        for b in range(NBLK):
            r = slice(b * BLK, (b + 1) * BLK)
            pre = pre_s[r] + nn(S[r], PQ[...])
            a, sl = silu_parts(pre)
            act[l, r] = a
            slope[l, r] = sl
            n, v = norm_parts(nn(a, weo[l]))
            nrm[l, r] = n
            inv[l, r] = v
            lv = live[r]
            ne = (e[r].astype(F32) + lv * n).astype(BF16)
            if l + 1 < L:
                e1[r] = ne
            m = jnp.sum((lv * ne.astype(F32)).reshape(PER, K, D), axis=1)
            msg[l, b * PER : (b + 1) * PER] = m.astype(BF16)
        loads[l, 3].wait()
        pre = td_own[...] + nn(msg[l], wni[l, D:])
        a, sl = silu_parts(pre)
        actn[l] = a
        slopen[l] = sl
        n, v = norm_parts(nn(a, wno[l]))
        nrmn[l] = n
        invn[l] = v
        if l + 1 < L:
            h1[...] = (h[...].astype(F32) + oc[...] * n).astype(BF16)

    forward(0, h0, e0)
    forward(1, h1, e1)

    bufs = iter(rest)
    G, C, RA, RB, T1, SB, T2, ZB = {}, {}, {}, {}, {}, {}, {}, {}
    for l in range(L):
        for c in range(3):
            names = (G, C, RA, RB, T1, SB, T2, ZB) if c < 2 else (G, C, RA, RB, T1, SB)
            for name in names:
                name[l, c] = next(bufs)

    def store_unit(l, kind, unit, val):
        per, base = ((3, 0), (1, 3), (2, 4), (1, 6))[kind]
        val = val.astype(BF16)
        for n in range(D // 16):
            at = unit * (D // 16) + n
            d, j = at // per, base + at % per
            dcore, dxl, dz = d % 2, (d // 2) % 2, d // 4
            c = [j in GROUPS[l][k] for k in range(3)].index(True)
            g = GROUPS[l][c].index(j)
            for dxh in range(2):
                for dy in range(4):
                    dx = 2 * dxh + dxl
                    place = ((dx, dy, dz), (dy, dx, dz), (dz, dx, dy))[c]
                    row = 16 * n + 8 * dxh
                    G[l, c][(dcore,) + place + (g,)] = val[row : row + 8, 128 * dy : 128 * dy + 128]


    def node_back(l, h):
        gout = norm_back(nrmn[l], invn[l], oc[...] * gh[...]).astype(BF16)
        gpre = (nt(gout, wno[l]) * slopen[l]).astype(BF16)
        gin = nt(gpre, wni[l])
        gh[...] = gh[...] + gin[:, 0:D]
        store_unit(l, 2, 0, tn(h[...], gpre))
        store_unit(l, 2, 1, tn(msg[l], gpre))
        store_unit(l, 3, 0, tn(actn[l], gout))
        return gin[:, D:]

    def edge_back(l, gm, e):
        for b in range(NBLK):
            r = slice(b * BLK, (b + 1) * BLK)
            lv = live[r]
            part = gm[b * PER : (b + 1) * PER]
            part = jnp.broadcast_to(part[:, None, :], (PER, K, D)).reshape(BLK, D)
            ge2 = ges[r] + lv * part
            g = norm_back(nrm[l, r], inv[l, r], lv * ge2).astype(BF16)
            gedge[r] = g
            gp = (nt(g, weo[l]) * slope[l, r]).astype(BF16)
            gpe[r] = gp
            new = ge2 + nt(gp, wei[l, 0:D])
            if l:
                ges[r] = new
            else:
                ge_out[r] = new.astype(BF16)

    def weights_a(l):
        td = tds.at[l]
        sums = nn(ST[...], gpe[...])
        td[...] = sums.astype(BF16)
        td_own[...] = sums[0:ND]
        first = push(td.at[pl.ds(ND, H)], tarr.at[l, pl.ds(H, H)], before)
        second = push(td.at[pl.ds(ND + H, H)], tarr.at[l, pl.ds(0, H)], after)
        store_unit(l, 1, 0, tn(act[l], gedge[...]))
        return first, second

    def weights_b(l, h, e):
        td = tds.at[l]
        store_unit(l, 0, 0, tn(e[...], gpe[...]))
        store_unit(l, 0, 1, tn(tab[l], td[0:128]))
        whole = 2 * D // (3 * 16) // 4
        sent = [[swap_part(l, c, pl.ds(0, whole))] for c in range(2)]
        store_unit(l, 0, 2, tn(h[...], td[128:192]))
        for c in range(2):
            sent[c].append(swap_part(l, c, pl.ds(whole, 8 - whole)))
        return sent

    def nodes_done(l, returned):
        td = tds.at[l]
        for m in returned:
            m.wait_recv()
        src = (td_own[...] + nn(SENDT[...], tarr[l])).astype(BF16)
        pre_s[0:ND] = nt(src, wei[l, D : 2 * D]) + nt(td[128:192], wei[l, 2 * D :])
        into = gh if l else gn_out

        @pl.loop(0, ND // 8)
        def _(i):
            r = pl.ds(pl.multiple_of(8 * i, 8), 8)
            into[r] = gh[r] + pre_s[r]

    pos = ((x, y), (y, x))

    def swap(l, c):
        return push(G[l, c].at[1 - core], C[l, c], partner)

    def swap_part(l, c, part):
        al = slice(None)
        return push(G[l, c].at[1 - core, al, al, part], C[l, c].at[al, al, part], partner)

    def settle(l, c, i, rows):
        for k in rows:
            G[l, c][core, i, k] = G[l, c][core, i, k] + C[l, c][i, k]

    def absorb(l, c, i, k, more):
        G[l, c][core, i, k] = G[l, c][core, i, k] + C[l, c][i, k] + more

    def total(l, c, i, k, one, two):
        own = G[l, c][core, i, k].astype(F32) + C[l, c][i, k].astype(F32)
        T1[l, c][k] = (own + (one.astype(F32) + two.astype(F32))).astype(BF16)

    def ring4(l, c, swapped):
        for m in swapped:
            m.wait_recv()
        ref, ra, rb = G[l, c], RA[l, c], RB[l, c]
        a = pos[c][0]
        r, o, q = (a + 1) % 4, (a + 2) % 4, (a + 3) % 4
        lo, hi = pl.ds(0, 2), pl.ds(2, 2)
        settle(l, c, o, (0, 1))
        m1r = push(ref.at[core, o, lo], ra.at[0], right[c])
        settle(l, c, o, (2, 3))
        m1l = push(ref.at[core, o, hi], ra.at[1], left[c])
        settle(l, c, r, (2, 3))
        m2r = push(ref.at[core, r, hi], rb.at[0, hi], right[c])
        settle(l, c, q, (0, 1))
        m2l = push(ref.at[core, q, lo], rb.at[1, lo], left[c])

        def relay():
            m1r.wait_recv()
            for i in range(2):
                absorb(l, c, r, i, ra[0, i])
            m3r = push(ref.at[core, r, lo], rb.at[0, lo], right[c])
            m1l.wait_recv()
            for i in range(2):
                absorb(l, c, q, 2 + i, ra[1, i])
            m3l = push(ref.at[core, q, hi], rb.at[1, hi], left[c])

            def close():
                for m in (m2r, m2l, m3r, m3l):
                    m.wait_recv()
                for i in range(4):
                    total(l, c, a, i, rb[0, i], rb[1, i])

            return close

        return relay

    def across(l, c):
        b = pos[c][1]
        t, s = T1[l, c], SB[l, c]
        peer = [plane[(0, o) if c == 0 else (o, 0)] for o in range(1, 4)]
        sent = [push(t.at[(b + o) % 4], s.at[o], peer[o - 1]) for o in range(1, 4)]

        def close():
            for m in sent:
                m.wait_recv()
            total = t[b].astype(F32)
            for o in range(1, 4):
                total = total + s[o].astype(F32)
            T2[l, c][...] = total.astype(BF16)

        return close

    def keep(l, c, total):
        for g, j in enumerate(GROUPS[l][c]):
            AG[l, me, j] = total[g].astype(BF16)

    def along(l, c):
        t, s = T2[l, c], ZB[l, c]
        sent = [push(t.at[(z + o) % 8], s.at[o], z_peers[o - 1]) for o in range(1, 8)]

        def close():
            for m in sent:
                m.wait_recv()
            total = t[z].astype(F32)
            for o in range(1, 8):
                total = total + s[o].astype(F32)
            keep(l, c, total)

        return close

    def ring8(l, swapped):
        swapped.wait_recv()
        ref, first, full = G[l, 2], RA[l, 2], RB[l, 2]
        lo, hi = pl.ds(0, 2), pl.ds(2, 2)
        far = (z + 4) % 8
        settle(l, 2, far, range(4))
        got = [
            push(ref.at[core, far, lo], first.at[0], right[2]),
            push(ref.at[core, far, hi], first.at[1], left[2]),
        ]

        def step(n):
            for way in range(2):
                at = (z + (4 - n if way == 0 else 4 + n)) % 8
                if n == 1:
                    settle(l, 2, at, (2 - 2 * way, 3 - 2 * way))
                got[way].wait_recv()
                for i in (2 * way, 2 * way + 1) if n == 1 else range(4):
                    absorb(l, 2, at, i, first[way, i % 2] if n == 1 else full[way, n - 2, i])
                got[way] = push(
                    ref.at[core, at], full.at[way, n - 1], (right, left)[way][2]
                )

        def close():
            for way in range(2):
                got[way].wait_recv()
            for i in range(4):
                total(l, 2, z, i, full[0, 2, i], full[1, 2, i])

        return step, close

    def spread_plane(l):
        t, s = T1[l, 2], SB[l, 2]
        sent = [
            push(t.at[(x + ox) % 4, (y + oy) % 4], s.at[ox, oy], dev) for (ox, oy), dev in plane.items()
        ]

        def close():
            for m in sent:
                m.wait_recv()
            total = t[x, y].astype(F32)
            for ox, oy in plane:
                total = total + s[ox, oy].astype(F32)
            keep(l, 2, total)

        return close

    def gather(l):
        return [push(AG.at[l, me], AG.at[l, me], peer) for peer in mesh_peers]

    def write(l, pushed):
        for m in pushed:
            m.wait_recv()
        wg_out[l] = AG[l]

    both = lambda fn, l: [fn(l, c) for c in range(2)]
    run = lambda fns: [fn() for fn in fns]

    drained = [0]

    def drain(upto):
        for copy in copies[drained[0] : upto]:
            copy.wait_send()
        drained[0] = upto

    gm = node_back(1, h1)
    swz1 = swap(1, 2)
    edge_back(1, gm, e1)
    z1, z1_close = ring8(1, swz1)
    back1 = weights_a(1)
    sw1 = weights_b(1, h1, e1)
    z1(1)
    nodes_done(1, back1)
    gm = node_back(0, h0)
    swz0 = swap(0, 2)
    z1(2)
    xy1 = [ring4(1, c, sw1[c]) for c in range(2)]
    edge_back(0, gm, e0)
    z1(3)
    xy1 = run(xy1)
    z0, z0_close = ring8(0, swz0)
    back0 = weights_a(0)
    run(xy1)
    xy1 = both(across, 1)
    z1_close()
    z1_end = spread_plane(1)
    sw0 = weights_b(0, h0, e0)
    early = len(copies)
    z0(1)
    run(xy1)
    xy1 = both(along, 1)
    xy0 = [ring4(0, c, sw0[c]) for c in range(2)]
    z0(2)
    z1_end()
    xy0 = run(xy0)
    run(xy1)
    last1 = gather(1)
    z0(3)
    drain(early)
    run(xy0)
    xy0 = both(across, 0)
    z0_close()
    z0_end = spread_plane(0)
    nodes_done(0, back0)
    write(1, last1)
    run(xy0)
    xy0 = both(along, 0)
    z0_end()
    drain(len(copies) - 14)
    run(xy0)
    last0 = gather(0)
    drain(len(copies) - 7)
    write(0, last0)
    drain(len(copies))


def body(
    node_feats, edge_feats, node_cot, edge_cot, w_edge_in, w_edge_out, w_node_in, w_node_out,
    neighbours, send_rows, edge_counts, ocean_mask,
):
    samples, nodes, features = node_feats.shape
    total_rows = samples * lax.axis_size("dp") * nodes * lax.axis_size("mesh")
    factor = 1.0 / total_rows**0.5
    vmem = pl.BlockSpec(memory_space=pltpu.VMEM)
    hbm = pl.BlockSpec(memory_space=pl.ANY)

    def buf(dtype, *shape):
        return pltpu.VMEM(shape, dtype)

    scratch = [
        buf(BF16, L, 3 * D, D), buf(BF16, L, D, D), buf(BF16, L, 2 * D, D), buf(BF16, L, D, D),
        pltpu.SemaphoreType.DMA((4 * L,)),
        buf(BF16, E, 192), buf(BF16, 192, E), buf(BF16, 2 * H, ND), buf(BF16, ND, 2 * H),
        buf(F32, E, 1), buf(F32, ND, 1), buf(BF16, 192, D), buf(F32, E, D),
        buf(BF16, L, E, D), buf(F32, L, E, D), buf(F32, L, E, D), buf(F32, L, E, 1),
        buf(BF16, E, D), buf(BF16, ND, D), buf(BF16, L, ND, D),
        buf(BF16, L, ND, D), buf(F32, L, ND, D), buf(F32, L, ND, D), buf(F32, L, ND, 1),
        buf(BF16, L, 2 * H, D), buf(BF16, L, 2 * H, D),
        buf(BF16, L, 192, D), buf(F32, ND, D), buf(BF16, L, 2 * H, D),
        buf(F32, ND, D), buf(F32, E, D), buf(BF16, E, D), buf(BF16, E, D), buf(BF16, L, 128, D),
        buf(BF16, L, 8, 7, 8, 128),
        pltpu.SemaphoreType.DMA((NSEM,)), pltpu.SemaphoreType.DMA((NSEM,)),
    ]
    for l in range(L):
        for c in range(3):
            tile = (len(GROUPS[l][c]), 8, 128)
            if c < 2:
                shapes = (
                    (2, 4, 4, 8), (4, 4, 8), (2, 2, 8), (2, 4, 8), (4, 8), (4, 8), (8,), (8,),
                )
            else:
                shapes = ((2, 8, 4, 4), (8, 4, 4), (2, 2, 4), (2, 3, 4, 4), (4, 4), (4, 4))
            scratch += [buf(BF16, *(shape + tile)) for shape in shapes]

    done = pl.pallas_call(
        kernel,
        out_shape=(
            jax.ShapeDtypeStruct((ND, D), F32),
            jax.ShapeDtypeStruct((E, D), BF16),
            jax.ShapeDtypeStruct((L, 8, 7, 8, 128), BF16),
        ),
        in_specs=[vmem] * 4 + [hbm] * 4 + [vmem] * 4,
        out_specs=(vmem,) * 3,
        scratch_shapes=scratch,
        compiler_params=pltpu.CompilerParams(
            collective_id=0, has_side_effects=True, vmem_limit_bytes=60 << 20
        ),
    )(
        node_feats.reshape(ND, D), edge_feats.reshape(E, D),
        node_cot.reshape(ND, D), edge_cot.reshape(E, D),
        w_edge_in, w_edge_out, w_node_in, w_node_out,
        neighbours.T, send_rows, edge_counts.reshape(1, ND), ocean_mask.reshape(1, ND),
    )

    def finish(gn, ge, wg, gn_out, ge_out, oei, oeo, oni, ono):
        gn_out[...] = gn[...]
        ge_out[...] = ge[...]
        for l in range(L):
            for j in range(7):
                ref, row = ((oei, j), (oei, j), (oei, j), (oeo, 0), (oni, 0), (oni, 1), (ono, 0))[j]
                for m in range(8):
                    r, q = 16 * row + 8 * (m % 2), 128 * (m // 2)
                    ref[l, r : r + 8, q : q + 128] = wg[l, m, j].astype(F32) * factor

    outs = pl.pallas_call(
        finish,
        out_shape=(
            jax.ShapeDtypeStruct((ND, D), F32),
            jax.ShapeDtypeStruct((E, D), BF16),
            jax.ShapeDtypeStruct((L, 48, D), F32),
            jax.ShapeDtypeStruct((L, 16, D), F32),
            jax.ShapeDtypeStruct((L, 32, D), F32),
            jax.ShapeDtypeStruct((L, 16, D), F32),
        ),
        in_specs=[vmem] * 3,
        out_specs=(vmem,) * 6,
    )(*done)
    return (outs[0].reshape(samples, nodes, D), outs[1].reshape(samples, nodes, K, D)) + tuple(outs[2:])


def solution(mesh):
    rows, edges = P("dp", "mesh", None), P("dp", "mesh", None, None)
    weight = P(None, "dp", None)
    return jax.shard_map(
        body,
        mesh=mesh,
        in_specs=(
            rows, edges, rows, edges, P(), P(), P(), P(),
            P("mesh", None), P("mesh", None), P("mesh"), P("mesh"),
        ),
        out_specs=(rows, edges, weight, weight, weight, weight),
        check_vma=False,
    )
```
